32 devices in a mesh: dp: 16 (over z, y, x), tensor: 2 (over core).
Axes of the slice: x: 2, y: 2, z: 4, core: 2. Of those that a mesh axis runs over, the one named last changes fastest.
Arguments:
- layer_input: bfloat16 [16, 1024, 768], P('dp', 'tensor'), may hold values from -6 to 6
- cotangent: bfloat16 [16, 1024, 768], P('dp', 'tensor'), may hold values from -6 to 6
- lengths: int32 [16], P('dp'), may hold values from 256 to 1024, as said below
- w_qkv: bfloat16 [2, 768, 3, 768], P(None, 'dp', None, 'tensor'), may hold values from -0.21875 to 0.21875
- w_out: bfloat16 [2, 768, 768], P(None, 'tensor', 'dp'), may hold values from -0.625 to 0.625
- w_up: bfloat16 [2, 768, 3072], P(None, 'dp', 'tensor'), may hold values from -0.21875 to 0.21875
- w_down: bfloat16 [2, 3072, 768], P(None, 'tensor', 'dp'), may hold values from -0.109375 to 0.109375
- vec_bias: float32 [2, 6, 768], P(None, None, ('dp', 'tensor')), may hold values from -2 to 2
- norm_gain: float32 [2, 2, 768], P(None, None, ('dp', 'tensor')), may hold values from 0.5 to 1.5
- bias_up: float32 [2, 3072], P(None, ('dp', 'tensor')), may hold values from -2 to 2
- seg_pos: float32 [8, 768], P(None, ('dp', 'tensor')), may hold values from -3 to 3
Outputs:
- output: bfloat16 [16, 1024, 768], P('dp', 'tensor')
- grad_input: float32 [16, 1024, 768], P('dp', 'tensor')
- grad_w_qkv: float32 [2, 768, 3, 768], P(None, 'dp', None, 'tensor')
- grad_w_out: float32 [2, 768, 768], P(None, 'tensor', 'dp')
- grad_w_up: float32 [2, 768, 3072], P(None, 'dp', 'tensor')
- grad_w_down: float32 [2, 3072, 768], P(None, 'tensor', 'dp')
- grad_vec_bias: float32 [2, 6, 768], P(None, None, ('dp', 'tensor'))
- grad_norm_gain: float32 [2, 2, 768], P(None, None, ('dp', 'tensor'))
- grad_bias_up: float32 [2, 3072], P(None, ('dp', 'tensor'))
- grad_seg_pos: float32 [8, 768], P(None, ('dp', 'tensor'))
The draws below stay inside these ranges and needn't reach their ends.
Inputs may be any that keep to these rules, and one draw needn't show every extreme that they name: `lengths`: valid slots are the first ones of a sequence; every draw holds a sequence of 1024 valid slots and one of 256.
All inputs are finite; a program needn't handle non-finite values.
Results may differ from the reference program's by a relative error of at most 0.02.
Values may be sent and summed in bfloat16 or wider, within the bound.
No kernel may reach another device: no remote copies, remote signals or barrier semaphores. Data moves between devices by JAX's collectives and lax.ppermute only.
A program may use at most 192 MiB of HBM per device.

```python
import jax
import jax.numpy as jnp
from jax import lax

D = 768
H = 12
HD = 64
FF = 3072
SEG = 128
LEN = 1024
NSEG = 8
SEQS = 16


def draw_lengths(key, part):
    first_key, second_key, third_key = jax.random.split(jax.random.fold_in(key, 17), 3)
    drawn = jax.random.randint(first_key, (SEQS,), LEN // 4, LEN + 1)
    full_pos = jax.random.randint(second_key, (), 0, SEQS)
    short_pos = (full_pos + 1 + jax.random.randint(third_key, (), 0, max(SEQS - 1, 1))) % SEQS
    drawn = drawn.at[short_pos].set(LEN // 4)
    drawn = drawn.at[full_pos].set(LEN)
    return drawn.astype(jnp.int32)


def levels(stream_key, extent, cuts, low, largest):
    def one(dim, parts):
        heights = jax.random.uniform(jax.random.fold_in(jax.random.fold_in(stream_key, 6), dim), (parts,), jnp.float32, low / len(cuts), largest / len(cuts))
        return jnp.repeat(jnp.exp(heights), extent[dim] // parts).reshape((-1,) + (1,) * (len(extent) - dim - 1))

    factor_of = one(*cuts[0])
    for cut in cuts[1:]:
        factor_of = factor_of * one(*cut)
    return factor_of


def bell_draw(stream_key, extent, deviation, reach, pieces=(), kind=jnp.bfloat16):
    values = deviation * jax.random.normal(stream_key, extent, jnp.float32)
    if pieces:
        values = values * levels(stream_key, extent, pieces, -0.22, 0.18)
    return jnp.clip(values, -reach, reach).astype(kind)


def setup_inputs(seed: int = 0) -> dict:
    key_list = jax.random.split(jax.random.key(seed), 12)
    layer_input = bell_draw(key_list[0], (SEQS, LEN, D), 1.0, 6.0, ((0, 16), (1, 2)))
    cotangent = bell_draw(key_list[1], (SEQS, LEN, D), 1.0, 6.0, ((0, 16), (1, 2)))
    lengths = draw_lengths(jax.random.fold_in(key_list[11], 71), 0)
    w_qkv = bell_draw(key_list[3], (2, D, 3, D), D ** -0.5, 0.21875, ((1, 16), (3, 2)))
    w_out = bell_draw(key_list[4], (2, D, D), (D // 8) ** -0.5, 0.625, ((1, 2), (2, 16)))
    w_up = bell_draw(key_list[5], (2, D, FF), D ** -0.5, 0.21875, ((1, 16), (2, 2)))
    w_down = bell_draw(key_list[6], (2, FF, D), FF ** -0.5, 0.109375, ((1, 2), (2, 16)))
    vec_bias = bell_draw(key_list[7], (2, 6, D), 0.3, 2.0, ((2, 32),), jnp.float32)
    norm_gain = jnp.clip(1.0 + 0.1 * jax.random.normal(key_list[8], (2, 2, D), jnp.float32), 0.5, 1.5)
    bias_up = bell_draw(key_list[9], (2, FF), 0.3, 2.0, ((1, 32),), jnp.float32)
    seg_pos = bell_draw(key_list[10], (NSEG, D), 0.5, 3.0, ((1, 32),), jnp.float32)
    return dict(layer_input=layer_input, cotangent=cotangent, lengths=lengths, w_qkv=w_qkv, w_out=w_out, w_up=w_up, w_down=w_down, vec_bias=vec_bias, norm_gain=norm_gain, bias_up=bias_up, seg_pos=seg_pos)


NEG_FILL = -1000000000.0
EPS_NORM = 1e-06
HIGH = lax.Precision.HIGHEST

@jax.custom_vjp
def low(v):
    return lax.optimization_barrier(v.astype(jnp.bfloat16)).astype(jnp.float32)

@jax.custom_vjp
def low_back(v):
    return v

def low_keep(v):
    return (low(v), None)

def low_pass(kept, grad):
    return (grad,)

def back_keep(v):
    return (v, None)

def back_low(kept, grad):
    return (low(grad),)
low.defvjp(low_keep, low_pass)
low_back.defvjp(back_keep, back_low)

def layer_norm(values, gain_vec, shift_vec):
    centred = values - lax.optimization_barrier(jnp.mean(values, axis=-1, keepdims=True))
    spread_sq = lax.optimization_barrier(jnp.mean(centred * centred, axis=-1, keepdims=True))
    return centred * lax.rsqrt(spread_sq + EPS_NORM) * gain_vec + shift_vec

def gelu_exact(values):
    return jax.nn.gelu(values, approximate=False)

def ref_block(rows, key_valid, param_set, index):
    w_qkv_all, w_out_all, w_up_all, w_down_all, vec_all, gain_all, up_all = param_set[:7]
    groups, width_rows, model_dim = rows.shape
    total_rows = groups * width_rows
    flat_in = rows.reshape(total_rows, model_dim)
    inp_low = low(flat_in)
    projected = jnp.einsum('nd,dke->nke', inp_low, w_qkv_all[index], precision=HIGH)
    query_r = low(low_back(projected[:, 0] + vec_all[index, 0]))
    key_r = low(low_back(projected[:, 1]))
    value_r = low(low_back(projected[:, 2] + vec_all[index, 1]))
    shape_four = (groups, width_rows, H, HD)
    scores = jnp.einsum('grhe,gshe->ghrs', query_r.reshape(shape_four), key_r.reshape(shape_four), precision=HIGH) * HD ** (-0.5)
    scores = low_back(scores)
    scores = jnp.where(key_valid[:, None, None, :], scores, NEG_FILL)
    peak_val = lax.optimization_barrier(jnp.max(scores, axis=-1, keepdims=True))
    expo_val = jnp.exp(scores - peak_val)
    probs = low(expo_val / lax.optimization_barrier(jnp.sum(expo_val, axis=-1, keepdims=True)))
    attended = jnp.einsum('ghrs,gshe->grhe', probs, value_r.reshape(shape_four), precision=HIGH).reshape(total_rows, model_dim)
    attended = low(low_back(attended))
    branch_out = low_back(jnp.dot(attended, w_out_all[index], precision=HIGH))
    first = layer_norm(branch_out + vec_all[index, 2] + flat_in, gain_all[index, 0], vec_all[index, 4])
    hidden_in = low(first)
    pre_act = low_back(jnp.dot(hidden_in, w_up_all[index], precision=HIGH) + up_all[index])
    activated = low(gelu_exact(pre_act))
    second_out = low_back(jnp.dot(activated, w_down_all[index], precision=HIGH))
    result = layer_norm(second_out + vec_all[index, 3] + first, gain_all[index, 1], vec_all[index, 5])
    return result.reshape(groups, width_rows, model_dim)

def forward(param_set, inputs, lengths_here):
    batch_count = inputs.shape[0]
    positions = jnp.arange(LEN, dtype=jnp.int32)
    valid = positions[None, :] < lengths_here[:, None]
    first_out = ref_block(inputs.reshape(batch_count * NSEG, SEG, D), valid.reshape(batch_count * NSEG, SEG), param_set, 0)
    first_out = first_out.reshape(batch_count, LEN, D)
    seg_valid = valid[:, ::SEG]
    cls_in = first_out[:, ::SEG, :] + param_set[7][None]
    cls_out = ref_block(cls_in, seg_valid, param_set, 1)
    combined = first_out.at[:, ::SEG, :].set(cls_out)
    return combined * valid[..., None].astype(jnp.float32)

def reference(layer_input, cotangent, lengths, w_qkv, w_out, w_up, w_down, vec_bias, norm_gain, bias_up, seg_pos):
    param_set = tuple((array_in.astype(jnp.float32) for array_in in (w_qkv, w_out, w_up, w_down, vec_bias, norm_gain, bias_up, seg_pos)))
    per_step = min(SEQS, max(1, 4096 // LEN))
    step_count = SEQS // per_step
    inputs = layer_input.astype(jnp.float32).reshape(step_count, per_step, LEN, D)
    cots = cotangent.astype(jnp.float32).reshape(step_count, per_step, LEN, D)
    lengths_all = lengths.reshape(step_count, per_step)
    zero_set = tuple((jnp.zeros_like(array_in) for array_in in param_set))

    def scan_step(carry_sum, scan_item):
        inp_here, cot_here, len_here = scan_item
        outputs_here, pull_back = jax.vjp(lambda weights_in, data_in: forward(weights_in, data_in, len_here), param_set, inp_here)
        grad_params, grad_data = pull_back(cot_here)
        carry_sum = tuple((summed + grad_part for summed, grad_part in zip(carry_sum, grad_params)))
        return (carry_sum, (outputs_here.astype(jnp.bfloat16), grad_data))
    totals, (outs_all, grads_all) = lax.scan(scan_step, zero_set, (inputs, cots, lengths_all))
    scale_one = float(SEQS * LEN) ** (-0.5)
    scale_two = float(SEQS * NSEG) ** (-0.5)
    block_scale = jnp.array([scale_one, scale_two], jnp.float32)
    scaled = tuple((totals[position] * block_scale.reshape((2,) + (1,) * (totals[position].ndim - 1)) for position in range(7)))
    grad_segment = totals[7] * jnp.float32(scale_two)
    return (outs_all.reshape(SEQS, LEN, D), grads_all.reshape(SEQS, LEN, D), scaled[0], scaled[1], scaled[2], scaled[3], scaled[4], scaled[5], scaled[6], grad_segment)
```

```python
import functools
import math

import jax
import jax.numpy as jnp
from jax import lax
from jax.experimental import pallas as pl
from jax.experimental.pallas import tpu as pltpu
from jax.sharding import PartitionSpec as P

HD = 64
SEG = 128
NEG_FILL = -1000000000.0
EPS_NORM = 1e-06
BF = jnp.bfloat16
F32 = jnp.float32
INV_SQRT2 = 1.0 / math.sqrt(2.0)
INV_SQRT2PI = 1.0 / math.sqrt(2.0 * math.pi)
SM_SCALE = HD ** (-0.5)


def dot_nn(a, b):
    return lax.dot_general(a, b, (((1,), (0,)), ((), ())), preferred_element_type=F32)


def dot_nt(a, b):
    return lax.dot_general(a, b, (((1,), (1,)), ((), ())), preferred_element_type=F32)


def dot_tn(a, b):
    return lax.dot_general(a, b, (((0,), (0,)), ((), ())), preferred_element_type=F32)


def dot_exact(a, b):
    return lax.dot_general(
        a, b, (((1,), (0,)), ((), ())), precision=lax.Precision.HIGHEST, preferred_element_type=F32
    )


def swap_dp(values, bit, count):
    return lax.ppermute(values, "dp", [(i, i ^ (1 << bit)) for i in range(count)])


def swap_tensor(values):
    return lax.ppermute(values, "tensor", [(0, 1), (1, 0)])


def bit_orders(bits):
    if bits == 4:
        return ((3, 0, 1, 2), (3, 1, 2, 0), (3, 2, 0, 1))
    base = tuple(range(bits))
    return (base, base[1:] + base[:1], base[2:] + base[:2])


def gather_step(values, bit, bits, count):
    return jnp.concatenate([values, swap_dp(values, bit, count)], axis=bits - 1 - bit)


def gather_units(units, orders, bits, count):
    state = [unit.reshape((1,) * bits + unit.shape) for unit in units]
    for step in range(bits):
        state = [gather_step(v, orders[i][step], bits, count) for i, v in enumerate(state)]
    return [v.reshape((-1, v.shape[-1])) for v in state]


def scatter_unit(grad, order, bits, count):
    width = grad.shape[-1]
    v = grad.reshape((2,) * bits + (-1, width))
    for step, bit in enumerate(reversed(order)):
        axis = bits - 1 - bit
        send = lax.index_in_dim(v, 1, axis, keepdims=True)
        keep = lax.index_in_dim(v, 0, axis, keepdims=True).astype(F32)
        v = keep + swap_dp(send, bit, count).astype(F32)
        if step < bits - 1:
            v = v.astype(BF)
    return v.reshape((-1, width))


def sum_everywhere(values, bits, count):
    values = values + swap_tensor(values)
    for bit in range(bits):
        values = values + swap_dp(values, bit, count)
    return values


def pair_masks(rows):
    lane = lax.broadcasted_iota(jnp.int32, (rows, 2 * HD), 1)
    return lane < HD


def stack_heads(two, low_half):
    zero = jnp.zeros_like(two)
    return jnp.concatenate([jnp.where(low_half, two, zero), jnp.where(low_half, zero, two)], axis=0)


def merge_heads(stacked, low_half, rows):
    return jnp.where(low_half, stacked[:rows], stacked[rows:])


def pair_probs(q_stack, key_two, allowed):
    scores = dot_nt(q_stack, key_two) * SM_SCALE
    scores = jnp.where(allowed, scores, NEG_FILL)
    expo = jnp.exp(scores - jnp.max(scores, axis=-1, keepdims=True))
    return expo * (1.0 / jnp.sum(expo, axis=-1, keepdims=True))


def attn_fwd_kernel(count_ref, qkv_ref, out_ref):
    rows = qkv_ref.shape[0]
    width = out_ref.shape[1]
    low_half = pair_masks(rows)
    allowed = lax.broadcasted_iota(jnp.int32, (2 * rows, rows), 1) < count_ref[pl.program_id(0)]
    for pair in range(width // (2 * HD)):
        at = pair * 2 * HD
        q_stack = stack_heads(qkv_ref[:, at : at + 2 * HD], low_half)
        probs = pair_probs(q_stack, qkv_ref[:, width + at : width + at + 2 * HD], allowed)
        mixed = dot_nn(probs.astype(BF), qkv_ref[:, 2 * width + at : 2 * width + at + 2 * HD])
        out_ref[:, at : at + 2 * HD] = merge_heads(mixed, low_half, rows).astype(BF)


def attn_bwd_kernel(count_ref, qkv_ref, grad_ref, out_ref, sums_ref):
    rows = qkv_ref.shape[0]
    width = grad_ref.shape[1]
    low_half = pair_masks(rows)
    allowed = lax.broadcasted_iota(jnp.int32, (2 * rows, rows), 1) < count_ref[pl.program_id(0)]

    @pl.when(pl.program_id(0) == 0)
    def _():
        sums_ref[...] = jnp.zeros_like(sums_ref)

    def put(at, values):
        low = values.astype(BF)
        out_ref[:, at : at + 2 * HD] = low
        sums_ref[:, at : at + 2 * HD] += jnp.sum(low.astype(F32), axis=0, keepdims=True)

    for pair in range(width // (2 * HD)):
        at = pair * 2 * HD
        q_stack = stack_heads(qkv_ref[:, at : at + 2 * HD], low_half)
        key_two = qkv_ref[:, width + at : width + at + 2 * HD]
        value_two = qkv_ref[:, 2 * width + at : 2 * width + at + 2 * HD]
        g_stack = stack_heads(grad_ref[:, at : at + 2 * HD], low_half)
        probs = pair_probs(q_stack, key_two, allowed)
        grad_probs = dot_nt(g_stack, value_two)
        inner = jnp.sum(grad_probs * probs, axis=-1, keepdims=True)
        grad_scores = jnp.where(allowed, probs * (grad_probs - inner), 0.0).astype(BF)
        put(at, merge_heads(dot_nn(grad_scores, key_two), low_half, rows) * SM_SCALE)
        put(width + at, dot_tn(grad_scores, q_stack) * SM_SCALE)
        put(2 * width + at, dot_tn(probs.astype(BF), g_stack))


def attn_fwd(counts, qkv):
    rows, three = qkv.shape
    width = three // 3
    return pl.pallas_call(
        attn_fwd_kernel,
        grid_spec=pltpu.PrefetchScalarGridSpec(
            num_scalar_prefetch=1,
            grid=(rows // SEG,),
            in_specs=[pl.BlockSpec((SEG, three), lambda i, c: (i, 0))],
            out_specs=pl.BlockSpec((SEG, width), lambda i, c: (i, 0)),
        ),
        out_shape=jax.ShapeDtypeStruct((rows, width), BF),
        cost_estimate=pl.CostEstimate(
            flops=8 * rows * SEG * width, bytes_accessed=8 * rows * width, transcendentals=rows * SEG * width // HD
        ),
        name="attn_fwd",
    )(counts, qkv)


def attn_bwd(counts, qkv, grad):
    rows, three = qkv.shape
    width = three // 3
    return pl.pallas_call(
        attn_bwd_kernel,
        grid_spec=pltpu.PrefetchScalarGridSpec(
            num_scalar_prefetch=1,
            grid=(rows // SEG,),
            in_specs=[
                pl.BlockSpec((SEG, three), lambda i, c: (i, 0)),
                pl.BlockSpec((SEG, width), lambda i, c: (i, 0)),
            ],
            out_specs=[
                pl.BlockSpec((SEG, three), lambda i, c: (i, 0)),
                pl.BlockSpec((1, three), lambda i, c: (0, 0)),
            ],
        ),
        out_shape=[jax.ShapeDtypeStruct((rows, three), BF), jax.ShapeDtypeStruct((1, three), F32)],
        cost_estimate=pl.CostEstimate(
            flops=20 * rows * SEG * width, bytes_accessed=14 * rows * width, transcendentals=rows * SEG * width // HD
        ),
        name="attn_bwd",
    )(counts, qkv, grad)


def gelu_pair(pre):
    cdf = 0.5 * (1.0 + lax.erf(pre * INV_SQRT2))
    return pre * cdf, cdf + pre * (jnp.exp(-0.5 * pre * pre) * INV_SQRT2PI)


def up_kernel(rows_ref, w_ref, bias_ref, act_ref, slope_ref):
    pre = dot_nn(rows_ref[...], w_ref[...]) + bias_ref[...]
    act, slope = gelu_pair(pre)
    act_ref[...] = act.astype(BF)
    slope_ref[...] = slope.astype(BF)


def up_gelu(rows, w_up, bias):
    total, dim = rows.shape
    hidden = w_up.shape[1]
    tile_r = min(256, total)
    tile_h = min(512, hidden)
    spec_out = pl.BlockSpec((tile_r, tile_h), lambda j, i: (i, j))
    return pl.pallas_call(
        up_kernel,
        grid=(hidden // tile_h, total // tile_r),
        in_specs=[
            pl.BlockSpec((tile_r, dim), lambda j, i: (i, 0)),
            pl.BlockSpec((dim, tile_h), lambda j, i: (0, j)),
            pl.BlockSpec((1, tile_h), lambda j, i: (0, j)),
        ],
        out_specs=[spec_out, spec_out],
        out_shape=[jax.ShapeDtypeStruct((total, hidden), BF)] * 2,
        cost_estimate=pl.CostEstimate(
            flops=2 * total * dim * hidden, bytes_accessed=4 * total * hidden, transcendentals=2 * total * hidden
        ),
        name="up_gelu",
    )(rows, w_up, bias[None, :])


def norm_stats(values):
    centred = values - jnp.mean(values, axis=-1, keepdims=True)
    inv = lax.rsqrt(jnp.mean(centred * centred, axis=-1, keepdims=True) + EPS_NORM)
    return centred * inv, inv


def norm_bwd(grad, unit, inv, gain):
    scaled = grad * gain
    along = jnp.mean(scaled * unit, axis=-1, keepdims=True)
    return inv * (scaled - jnp.mean(scaled, axis=-1, keepdims=True) - unit * along)


def column_sum(values):
    return jnp.sum(values, axis=0)


def local(
    layer_input,
    cotangent,
    lengths,
    w_qkv,
    w_out,
    w_up,
    w_down,
    vec_bias,
    norm_gain,
    bias_up,
    seg_pos,
):
    count = lax.axis_size("dp")
    bits = count.bit_length() - 1
    me = lax.axis_index("dp")
    part = lax.axis_index("tensor")
    seqs_here, half, dim = layer_input.shape
    full_len = 2 * half
    segments = full_len // SEG
    seg_half = half // SEG
    chunk = dim // count
    width = w_qkv.shape[3]
    hidden = w_up.shape[2]
    orders = bit_orders(bits)
    swap_half = swap_tensor

    row_id = lax.broadcasted_iota(jnp.int32, (dim, dim), 0)
    col_id = lax.broadcasted_iota(jnp.int32, (dim, dim), 1)
    perm_hot = row_id == ((col_id // chunk) ^ me) * chunk + col_id % chunk
    perm = perm_hot.astype(BF)
    perm_f = perm_hot.astype(F32)

    def shards(block):
        return [
            jnp.concatenate([w_qkv[block].reshape(chunk, 3 * width), w_out[block].T], axis=1),
            w_up[block],
            w_down[block].T,
        ]

    units_one = gather_units(shards(0), orders, bits, count)
    second = shards(1)
    units_two = gather_units(
        [lax.optimization_barrier((s, units_one[0]))[0] for s in second], orders, bits, count
    )

    slot = me * 2 + part
    piece = vec_bias.shape[2]
    place = (
        lax.broadcasted_iota(jnp.int32, (piece, dim), 1)
        == lax.broadcasted_iota(jnp.int32, (piece, dim), 0) + slot * piece
    ).astype(F32)
    piece_up = bias_up.shape[1]
    hidden_all = piece_up * count * 2
    place_up = (
        lax.broadcasted_iota(jnp.int32, (piece_up, hidden_all), 1)
        == lax.broadcasted_iota(jnp.int32, (piece_up, hidden_all), 0) + slot * piece_up
    ).astype(F32)
    small_rows = jnp.concatenate(
        [vec_bias.reshape(-1, piece), norm_gain.reshape(-1, piece), seg_pos], axis=0
    )
    small = dot_exact(small_rows, place)
    small_up = dot_exact(bias_up, place_up)
    fold = hidden_all // dim
    small_all = sum_everywhere(
        jnp.concatenate([small, small_up.reshape(2 * fold, dim)], axis=0), bits, count
    )
    plain = small_all[: small_rows.shape[0]]
    up_all = small_all[small_rows.shape[0] :].reshape(2, 2, hidden)
    rel = dot_exact(plain, perm_f)

    def own_width(row):
        return jnp.where(part == 0, row[:width], row[width:])

    def block_vectors(block):
        base = 6 * block
        bias_qkv = jnp.concatenate(
            [own_width(plain[base]), jnp.zeros((width,), F32), own_width(plain[base + 1])]
        )
        hidden_bias = jnp.where(part == 0, up_all[block, 0], up_all[block, 1])
        gain_at = 12 + 2 * block
        return dict(
            qkv=bias_qkv,
            attn=rel[base + 2],
            mlp=rel[base + 3],
            shift_one=rel[base + 4],
            shift_two=rel[base + 5],
            gain_one=rel[gain_at],
            gain_two=rel[gain_at + 1],
            hidden=hidden_bias,
        )

    vec_one, vec_two = block_vectors(0), block_vectors(1)
    seg_rows = rel[16 : 16 + segments]

    length = lengths[0]
    seg_ids = jnp.concatenate(
        [part * seg_half + jnp.arange(seg_half), (1 - part) * seg_half + jnp.arange(seg_half)]
    ).astype(jnp.int32)
    seg_counts = jnp.clip(length - seg_ids * SEG, 0, SEG).astype(jnp.int32)

    def three_mats(units):
        return units[0][:, : 3 * width], units[0][:, 3 * width :], units[1], units[2]

    w_qkv_r, w_out_r, w_up_r, w_down_r = three_mats(units_one)
    x_own = dot_nn(layer_input[0], perm).astype(BF)
    x_full = jnp.concatenate([x_own, swap_half(x_own)], axis=0)
    qkv = (dot_nn(x_full, w_qkv_r) + vec_one["qkv"]).astype(BF)
    attended = attn_fwd(seg_counts, qkv)
    partial_attn = dot_nt(attended, w_out_r).astype(BF)
    first_sum = (
        partial_attn[:half].astype(F32)
        + swap_half(partial_attn[half:]).astype(F32)
        + vec_one["attn"]
        + x_own.astype(F32)
    )
    unit_one, inv_one = norm_stats(first_sum)
    first = unit_one * vec_one["gain_one"] + vec_one["shift_one"]
    first_low = first.astype(BF)
    first_full = jnp.concatenate([first_low, swap_half(first_low)], axis=0)
    act, slope = up_gelu(first_full, w_up_r, vec_one["hidden"])
    partial_mlp = dot_nt(act, w_down_r).astype(BF)
    second_sum = (
        partial_mlp[:half].astype(F32) + swap_half(partial_mlp[half:]).astype(F32) + vec_one["mlp"] + first
    )
    unit_two, inv_two = norm_stats(second_sum)
    first_out = unit_two * vec_one["gain_two"] + vec_one["shift_two"]

    v2 = vec_two
    y_qkv, y_out, y_up, y_down = three_mats(units_two)

    def both_halves(own_rows):
        other = swap_half(own_rows)
        return jnp.where(
            part == 0,
            jnp.concatenate([own_rows, other], axis=0),
            jnp.concatenate([other, own_rows], axis=0),
        )

    def own_half(rows):
        return jnp.where(part == 0, rows[:seg_half], rows[seg_half:])

    cls_own = first_out.reshape(seg_half, SEG, dim)[:, 0]
    cls_in = both_halves(cls_own) + seg_rows
    cls_low = cls_in.astype(BF)
    key_ok = (jnp.arange(segments) * SEG < length)[None, None, :]
    qkv_c = (dot_nn(cls_low, y_qkv) + v2["qkv"]).astype(BF)
    heads = width // HD
    q_c, k_c, v_c = (qkv_c[:, i * width : (i + 1) * width].reshape(segments, heads, HD) for i in range(3))
    scores_c = jnp.einsum("rhe,she->hrs", q_c, k_c, preferred_element_type=F32) * SM_SCALE
    scores_c = jnp.where(key_ok, scores_c, NEG_FILL)
    expo_c = jnp.exp(scores_c - jnp.max(scores_c, axis=-1, keepdims=True))
    probs_c = expo_c / jnp.sum(expo_c, axis=-1, keepdims=True)
    probs_c_low = probs_c.astype(BF)
    att_c = (
        jnp.einsum("hrs,she->rhe", probs_c_low, v_c, preferred_element_type=F32)
        .astype(BF)
        .reshape(segments, width)
    )
    part_c = dot_nt(att_c, y_out)
    sum_c1 = part_c + swap_half(part_c) + v2["attn"] + cls_in
    unit_c1, inv_c1 = norm_stats(sum_c1)
    first_c = unit_c1 * v2["gain_one"] + v2["shift_one"]
    first_c_low = first_c.astype(BF)
    act_f, slope_c = gelu_pair(dot_nn(first_c_low, y_up) + v2["hidden"])
    act_c = act_f.astype(BF)
    part_c2 = dot_nt(act_c, y_down)
    sum_c2 = part_c2 + swap_half(part_c2) + v2["mlp"] + first_c
    unit_c2, inv_c2 = norm_stats(sum_c2)
    cls_out = unit_c2 * v2["gain_two"] + v2["shift_two"]

    row_in = lax.broadcasted_iota(jnp.int32, (half, 1), 0)
    valid = part * half + row_in < length
    is_cls = (lax.broadcasted_iota(jnp.int32, (1, SEG, 1), 1) == 0)

    def with_cls(rows, cls):
        return jnp.where(is_cls, cls[:, None, :], rows.reshape(seg_half, SEG, dim)).reshape(half, dim)

    combined = jnp.where(valid, with_cls(first_out, own_half(cls_out)), 0.0).astype(BF)
    output = dot_nn(combined, perm).astype(BF)[None]

    cot = jnp.where(valid, cotangent[0], jnp.zeros_like(cotangent[0]))
    grad_y_low = dot_nn(cot, perm).astype(BF)
    cot_cls = grad_y_low.reshape(seg_half, SEG, dim)[:, 0]
    g_c = both_halves(cot_cls).astype(F32)
    g_second_c = norm_bwd(g_c, unit_c2, inv_c2, v2["gain_two"])
    g_mlp_c = g_second_c.astype(BF)
    gpre_c = (dot_nn(g_mlp_c, y_down) * slope_c).astype(BF)
    gw_down_c = dot_tn(g_mlp_c, act_c).astype(BF)
    gw_up_c = dot_tn(first_c_low, gpre_c).astype(BF)
    part_g1 = dot_nt(gpre_c, y_up)
    g_first_c = part_g1 + swap_half(part_g1) + g_second_c
    g_sum_c = norm_bwd(g_first_c, unit_c1, inv_c1, v2["gain_one"])
    g_attn_c = g_sum_c.astype(BF)
    gw_out_c = dot_tn(g_attn_c, att_c).astype(BF)
    g_att_c = dot_nn(g_attn_c, y_out).astype(BF).reshape(segments, heads, HD)
    gv_c = jnp.einsum("hrs,rhe->she", probs_c_low, g_att_c, preferred_element_type=F32)
    gp_c = jnp.einsum("rhe,she->hrs", g_att_c, v_c, preferred_element_type=F32)
    in_c = jnp.sum(gp_c * probs_c, axis=-1, keepdims=True)
    gs_c = jnp.where(key_ok, probs_c * (gp_c - in_c), 0.0).astype(BF)
    gq_c = jnp.einsum("hrs,she->rhe", gs_c, k_c, preferred_element_type=F32) * SM_SCALE
    gk_c = jnp.einsum("hrs,rhe->she", gs_c, q_c, preferred_element_type=F32) * SM_SCALE
    gqkv_c = jnp.concatenate([g.reshape(segments, width) for g in (gq_c, gk_c, gv_c)], axis=1).astype(BF)
    gw_qkv_c = dot_tn(cls_low, gqkv_c).astype(BF)
    part_g2 = dot_nt(gqkv_c, y_qkv)
    g_cls_in = part_g2 + swap_half(part_g2) + g_sum_c

    grad_out = with_cls(grad_y_low.astype(F32), own_half(g_cls_in))
    g_second = norm_bwd(grad_out, unit_two, inv_two, vec_one["gain_two"])
    g_second_low = g_second.astype(BF)
    g_mlp = jnp.concatenate([g_second_low, swap_half(g_second_low)], axis=0)
    gpre = (dot_nn(g_mlp, w_down_r) * slope.astype(F32)).astype(BF)
    gw_down = dot_tn(g_mlp, act).astype(BF)
    part_h = dot_nt(gpre, w_up_r).astype(BF)
    gw_up = dot_tn(first_full, gpre).astype(BF)
    g_first = part_h[:half].astype(F32) + swap_half(part_h[half:]).astype(F32) + g_second
    g_first_sum = norm_bwd(g_first, unit_one, inv_one, vec_one["gain_one"])
    g_first_low = g_first_sum.astype(BF)
    g_attn = jnp.concatenate([g_first_low, swap_half(g_first_low)], axis=0)
    gw_out = dot_tn(g_attn, attended).astype(BF)
    g_attended = dot_nn(g_attn, w_out_r).astype(BF)
    gqkv, gqkv_sums = attn_bwd(seg_counts, qkv, g_attended)
    part_x = dot_nt(gqkv, w_qkv_r).astype(BF)
    gw_qkv = dot_tn(x_full, gqkv).astype(BF)
    g_in = part_x[:half].astype(F32) + swap_half(part_x[half:]).astype(F32) + g_first_sum
    g_in_high = lax.reduce_precision(g_in, 8, 7)
    grad_input = (dot_nn(g_in_high.astype(BF), perm) + dot_nn((g_in - g_in_high).astype(BF), perm))[None]

    scale_one = 1.0 / math.sqrt(seqs_here * count * full_len)
    scale_two = 1.0 / math.sqrt(seqs_here * count * segments)

    def reduced(first_grad, second_grad, order):
        return (
            scatter_unit(first_grad, order, bits, count) * scale_one,
            scatter_unit(second_grad, order, bits, count) * scale_two,
        )

    down_one, down_two = reduced(gw_down, gw_down_c, orders[2])
    up_one, up_two = reduced(gw_up, gw_up_c, orders[1])
    out_one, out_two = reduced(gw_out, gw_out_c, orders[0])
    qkv_one, qkv_two = reduced(gw_qkv, gw_qkv_c, orders[0])
    grad_w_qkv = jnp.stack([qkv_one, qkv_two]).reshape(2, chunk, 3, width)
    grad_w_out = jnp.stack([out_one.T, out_two.T])
    grad_w_up = jnp.stack([up_one, up_two])
    grad_w_down = jnp.stack([down_one.T, down_two.T])

    def spread(values, total):
        zero = jnp.zeros((total - values.shape[0],), F32)
        return jnp.where(part == 0, jnp.concatenate([values, zero]), jnp.concatenate([zero, values]))

    rel_rows = jnp.stack(
        [
            column_sum(g_first_sum) * scale_one,
            column_sum(g_second) * scale_one,
            column_sum(g_first) * scale_one,
            column_sum(grad_out) * scale_one,
            column_sum(own_half(g_sum_c)) * scale_two,
            column_sum(own_half(g_second_c)) * scale_two,
            column_sum(own_half(g_first_c)) * scale_two,
            column_sum(own_half(g_c)) * scale_two,
            column_sum(g_first * unit_one) * scale_one,
            column_sum(grad_out * unit_two) * scale_one,
            column_sum(own_half(g_first_c * unit_c1)) * scale_two,
            column_sum(own_half(g_c * unit_c2)) * scale_two,
        ]
    )
    zeros_half = jnp.zeros((seg_half, dim), F32)
    cls_part = own_half(g_cls_in) * scale_two
    seg_grad = jnp.where(
        part == 0,
        jnp.concatenate([cls_part, zeros_half], axis=0),
        jnp.concatenate([zeros_half, cls_part], axis=0),
    )
    canon = dot_exact(jnp.concatenate([rel_rows, seg_grad], axis=0), perm_f)
    sums_c = column_sum(gqkv_c.astype(F32)) * scale_two
    sums_o = gqkv_sums[0] * scale_one
    bias_rows = jnp.stack(
        [
            spread(sums_o[:width], dim),
            spread(sums_o[2 * width :], dim),
            canon[0],
            canon[1],
            canon[2],
            canon[3],
            spread(sums_c[:width], dim),
            spread(sums_c[2 * width :], dim),
            canon[4],
            canon[5],
            canon[6],
            canon[7],
        ]
    )
    up_rows = jnp.stack(
        [
            spread(column_sum(gpre.astype(F32)) * scale_one, hidden_all),
            spread(column_sum(gpre_c.astype(F32)) * scale_two, hidden_all),
        ]
    )
    all_small = sum_everywhere(
        jnp.concatenate([bias_rows, canon[8:], up_rows.reshape(2 * fold, dim)], axis=0), bits, count
    )
    mine = dot_exact(all_small[:24], place.T)
    grad_vec = mine[:12].reshape(2, 6, piece)
    grad_gain = mine[12:16].reshape(2, 2, piece)
    grad_seg = mine[16:24]
    grad_up_vec = dot_exact(all_small[24:].reshape(2, hidden_all), place_up.T)
    return (
        output,
        grad_input,
        grad_w_qkv,
        grad_w_out,
        grad_w_up,
        grad_w_down,
        grad_vec,
        grad_gain,
        grad_up_vec,
        grad_seg,
    )


def solution(mesh):
    return jax.shard_map(
        local,
        mesh=mesh,
        in_specs=(
            P("dp", "tensor", None),
            P("dp", "tensor", None),
            P("dp"),
            P(None, "dp", None, "tensor"),
            P(None, "tensor", "dp"),
            P(None, "dp", "tensor"),
            P(None, "tensor", "dp"),
            P(None, None, ("dp", "tensor")),
            P(None, None, ("dp", "tensor")),
            P(None, ("dp", "tensor")),
            P(None, ("dp", "tensor")),
        ),
        out_specs=(
            P("dp", "tensor", None),
            P("dp", "tensor", None),
            P(None, "dp", None, "tensor"),
            P(None, "tensor", "dp"),
            P(None, "dp", "tensor"),
            P(None, "tensor", "dp"),
            P(None, None, ("dp", "tensor")),
            P(None, None, ("dp", "tensor")),
            P(None, ("dp", "tensor")),
            P(None, ("dp", "tensor")),
        ),
        check_vma=False,
    )
```

```python
import functools
import math

import jax
import jax.numpy as jnp
import numpy as np
from jax import lax
from jax.experimental import pallas as pl
from jax.experimental.pallas import tpu as pltpu
from jax.sharding import PartitionSpec as P

HD = 64
SEG = 128
NEG_FILL = -1000000000.0
EPS_NORM = 1e-06
BF = jnp.bfloat16
F32 = jnp.float32
INV_SQRT2 = 1.0 / math.sqrt(2.0)
INV_SQRT2PI = 1.0 / math.sqrt(2.0 * math.pi)
SM_SCALE = HD ** (-0.5)
PAIR = 2 * HD
PIECES = 3
BRIEF = pl.CostEstimate(flops=1, bytes_accessed=1, transcendentals=0)


def dot_nn(a, b):
    return lax.dot_general(a, b, (((1,), (0,)), ((), ())), preferred_element_type=F32)


def dot_nt(a, b):
    return lax.dot_general(a, b, (((1,), (1,)), ((), ())), preferred_element_type=F32)


def dot_tn(a, b):
    return lax.dot_general(a, b, (((0,), (0,)), ((), ())), preferred_element_type=F32)


def dot_exact(a, b):
    return lax.dot_general(
        a, b, (((1,), (0,)), ((), ())), precision=lax.Precision.HIGHEST, preferred_element_type=F32
    )


def swap_dp(values, bit, count):
    return lax.ppermute(values, "dp", [(i, i ^ (1 << bit)) for i in range(count)])


def swap_tensor(values):
    return lax.ppermute(values, "tensor", [(0, 1), (1, 0)])


def bit_orders(bits):
    if bits == 4:
        return ((3, 2, 0, 1), (3, 1, 2, 0), (3, 0, 1, 2))
    base = tuple(range(bits))
    return (base, base[1:] + base[:1], base[2:] + base[:2])


def tie(*values):
    return lax.optimization_barrier(values)


def join(low, high, bit, bits):
    return jnp.concatenate([low, high], axis=bits - 1 - bit)


class Gather:
    def __init__(self, pieces, orders, bits, count):
        self.state = [u.reshape((1,) * bits + u.shape) for u in pieces]
        self.orders, self.bits, self.count, self.step = orders, bits, count, 0

    def send(self):
        self.flying = [
            swap_dp(v, self.orders[i][self.step], self.count) for i, v in enumerate(self.state)
        ]

    def land(self):
        self.state = [
            join(v, f, self.orders[i][self.step], self.bits)
            for i, (v, f) in enumerate(zip(self.state, self.flying))
        ]
        self.step += 1

    def left(self):
        return self.bits - self.step

    def results(self):
        return [v.reshape((-1, v.shape[-1])) for v in self.state]


def half_of(values, axis, index):
    return lax.index_in_dim(values, index, axis, keepdims=True)


class Scatter:
    def __init__(self, pieces, orders, bits, count):
        self.bits, self.count, self.step = bits, count, 0
        self.orders = [tuple(reversed(o)) for o in orders]
        self.parts = [[[m.reshape((2,) * bits + (-1, m.shape[-1])) for m in piece]] for piece in pieces]

    def half(self, which, index):
        axis = self.bits - 1 - self.orders[which][self.step]
        cut = [
            jnp.concatenate([half_of(m, axis, index) for m in part], axis=-1).astype(F32)
            for part in self.parts[which]
        ]
        return sum(cut[1:], cut[0]).astype(BF)

    def prepare(self):
        self.leaving = [self.half(i, 1) for i in range(len(self.parts))]

    def send(self):
        self.flying = [
            swap_dp(v, self.orders[i][self.step], self.count) for i, v in enumerate(self.leaving)
        ]
        self.kept = [self.half(i, 0) for i in range(len(self.parts))]

    def land(self):
        self.parts = [[[k], [f]] for k, f in zip(self.kept, self.flying)]
        self.step += 1

    def left(self):
        return self.bits - self.step

    def pairs(self):
        return [side[0].reshape((-1, side[0].shape[-1])) for part in self.parts for side in part]


def settle(anchor, *moving):
    flat = [f for m in moving for f in m.flying]
    anchor, *flat = tie(anchor, *flat)
    for m in moving:
        m.flying = flat[: len(m.flying)]
        flat = flat[len(m.flying) :]
        m.land()
    return anchor


def launch(anchor, *moving):
    for m in moving:
        if isinstance(m, Scatter):
            m.prepare()
            anchor, *m.leaving = tie(anchor, *m.leaving)
        elif isinstance(m, Gather):
            anchor, *m.state = tie(anchor, *m.state)
        else:
            anchor, m.state = tie(anchor, m.state)
        m.send()
    return anchor


def pair_masks(rows):
    lane = lax.broadcasted_iota(jnp.int32, (rows, PAIR), 1)
    return lane < HD


def stack_heads(two, low_half):
    zero = jnp.zeros_like(two)
    return jnp.concatenate([jnp.where(low_half, two, zero), jnp.where(low_half, zero, two)], axis=0)


def merge_heads(stacked, low_half, rows):
    return jnp.where(low_half, stacked[:rows], stacked[rows:])


def pair_probs(q_stack, key_two, allowed):
    scores = dot_nt(q_stack, key_two) * SM_SCALE
    scores = jnp.where(allowed, scores, NEG_FILL)
    expo = jnp.exp(scores - jnp.max(scores, axis=-1, keepdims=True))
    return expo * (1.0 / jnp.sum(expo, axis=-1, keepdims=True))


def row_window(rows):
    return [pl.BlockSpec((SEG, cols), lambda i, c: (i, 0)) for cols in rows]


def attn_fwd_kernel(count_ref, qkv_ref, out_ref):
    rows = qkv_ref.shape[0]
    low_half = pair_masks(rows)
    allowed = lax.broadcasted_iota(jnp.int32, (2 * rows, rows), 1) < count_ref[pl.program_id(0)]
    for pair in range(out_ref.shape[1] // PAIR):
        at = 3 * pair * PAIR
        q_stack = stack_heads(qkv_ref[:, at : at + PAIR], low_half)
        probs = pair_probs(q_stack, qkv_ref[:, at + PAIR : at + 2 * PAIR], allowed)
        mixed = dot_nn(probs.astype(BF), qkv_ref[:, at + 2 * PAIR : at + 3 * PAIR])
        out_ref[:, pair * PAIR : (pair + 1) * PAIR] = merge_heads(mixed, low_half, rows).astype(BF)


def pair_bwd(qkv, grad, allowed, low_half):
    rows = grad.shape[0]
    key_two = qkv[:, PAIR : 2 * PAIR]
    q_stack = stack_heads(qkv[:, :PAIR], low_half)
    g_stack = stack_heads(grad, low_half)
    probs = pair_probs(q_stack, key_two, allowed)
    grad_probs = dot_nt(g_stack, qkv[:, 2 * PAIR :])
    inner = jnp.sum(grad_probs * probs, axis=-1, keepdims=True)
    grad_scores = jnp.where(allowed, probs * (grad_probs - inner), 0.0).astype(BF)
    return (
        merge_heads(dot_nn(grad_scores, key_two), low_half, rows) * SM_SCALE,
        dot_tn(grad_scores, q_stack) * SM_SCALE,
        dot_tn(probs.astype(BF), g_stack),
    )


def attn_bwd_kernel(count_ref, qkv_ref, grad_ref, first_ref, out_ref, sums_ref):
    rows = qkv_ref.shape[0]
    low_half = pair_masks(rows)
    allowed = lax.broadcasted_iota(jnp.int32, (2 * rows, rows), 1) < count_ref[pl.program_id(0)]
    is_first = lax.broadcasted_iota(jnp.int32, (rows, PAIR), 0) == 0

    @pl.when(pl.program_id(0) == 0)
    def _():
        sums_ref[...] = jnp.zeros_like(sums_ref)

    for pair in range(grad_ref.shape[1] // PAIR):
        at = 3 * pair * PAIR
        span = slice(pair * PAIR, (pair + 1) * PAIR)
        grad = jnp.where(is_first, first_ref[0, :, span], grad_ref[:, span].astype(F32)).astype(BF)
        for k, values in enumerate(pair_bwd(qkv_ref[:, at : at + 3 * PAIR], grad, allowed, low_half)):
            low = values.astype(BF)
            to = slice(at + k * PAIR, at + (k + 1) * PAIR)
            out_ref[:, to] = low
            sums_ref[:, to] += jnp.sum(low.astype(F32), axis=0, keepdims=True)


def attn_fwd(counts, qkv):
    rows, three = qkv.shape
    width = three // 3
    return pl.pallas_call(
        attn_fwd_kernel,
        grid_spec=pltpu.PrefetchScalarGridSpec(
            num_scalar_prefetch=1,
            grid=(rows // SEG,),
            in_specs=row_window([three]),
            out_specs=row_window([width])[0],
        ),
        out_shape=jax.ShapeDtypeStruct((rows, width), BF),
        cost_estimate=BRIEF,
        name="attn_fwd",
    )(counts, qkv)


def attn_bwd(counts, qkv, grad, grad_first):
    rows, three = qkv.shape
    width = three // 3
    return pl.pallas_call(
        attn_bwd_kernel,
        grid_spec=pltpu.PrefetchScalarGridSpec(
            num_scalar_prefetch=1,
            grid=(rows // SEG,),
            in_specs=row_window([three, width]) + [pl.BlockSpec((1, 1, width), lambda i, c: (i, 0, 0))],
            out_specs=row_window([three]) + [pl.BlockSpec((1, three), lambda i, c: (0, 0))],
        ),
        out_shape=[jax.ShapeDtypeStruct((rows, three), BF), jax.ShapeDtypeStruct((1, three), F32)],
        cost_estimate=BRIEF,
        name="attn_bwd",
    )(counts, qkv, grad, grad_first.astype(F32)[:, None, :])


def gelu_pair(pre):
    cdf = 0.5 * (1.0 + lax.erf(pre * INV_SQRT2))
    return pre * cdf, cdf + pre * (jnp.exp(-0.5 * pre * pre) * INV_SQRT2PI)


def up_kernel(rows_ref, w_ref, bias_ref, act_ref, slope_ref):
    act, slope = gelu_pair(dot_nn(rows_ref[...], w_ref[...]) + bias_ref[...])
    act_ref[...] = act.astype(BF)
    slope_ref[...] = slope.astype(BF)


def up_gelu(rows, w_up, bias):
    total, dim = rows.shape
    hidden = w_up.shape[1]
    tile_r = min(256, total)
    tile_h = min(512, hidden)
    spec_out = pl.BlockSpec((tile_r, tile_h), lambda j, i: (i, j))
    return pl.pallas_call(
        up_kernel,
        grid=(hidden // tile_h, total // tile_r),
        in_specs=[
            pl.BlockSpec((tile_r, dim), lambda j, i: (i, 0)),
            pl.BlockSpec((dim, tile_h), lambda j, i: (0, j)),
            pl.BlockSpec((1, tile_h), lambda j, i: (0, j)),
        ],
        out_specs=[spec_out, spec_out],
        out_shape=[jax.ShapeDtypeStruct((total, hidden), BF)] * 2,
        cost_estimate=BRIEF,
        name="up_gelu",
    )(rows, w_up, bias[None, :])


def cls_attn_kernel(count_ref, rows_ref, w0, w1, w2, bias_ref, qkv_ref, att_ref, sum_ref):
    rows = rows_ref.shape[0]
    low_half = pair_masks(rows)
    allowed = lax.broadcasted_iota(jnp.int32, (2 * rows, rows), 1) < count_ref[0]
    total = jnp.zeros(sum_ref.shape, F32)
    for p, w in enumerate((w0, w1, w2)):
        span = slice(3 * p * PAIR, 3 * (p + 1) * PAIR)
        qkv = (dot_nn(rows_ref[...], w[:, : 3 * PAIR]) + bias_ref[:, span]).astype(BF)
        qkv_ref[:, span] = qkv
        probs = pair_probs(stack_heads(qkv[:, :PAIR], low_half), qkv[:, PAIR : 2 * PAIR], allowed)
        att = merge_heads(dot_nn(probs.astype(BF), qkv[:, 2 * PAIR :]), low_half, rows).astype(BF)
        att_ref[:, p * PAIR : (p + 1) * PAIR] = att[: att_ref.shape[0]]
        total += dot_nt(att, w[:, 3 * PAIR :])
    sum_ref[...] = total


def cls_attn_back_kernel(count_ref, grad_ref, w0, w1, w2, qkv_ref, out_ref, sum_ref):
    rows = grad_ref.shape[0]
    low_half = pair_masks(rows)
    allowed = lax.broadcasted_iota(jnp.int32, (2 * rows, rows), 1) < count_ref[0]
    total = jnp.zeros(sum_ref.shape, F32)
    for p, w in enumerate((w0, w1, w2)):
        span = slice(3 * p * PAIR, 3 * (p + 1) * PAIR)
        grad = dot_nn(grad_ref[...], w[:, 3 * PAIR :]).astype(BF)
        low = jnp.concatenate(pair_bwd(qkv_ref[:, span], grad, allowed, low_half), axis=1).astype(BF)
        out_ref[:, span] = low[: out_ref.shape[0]]
        total += dot_nt(low, w[:, : 3 * PAIR])
    sum_ref[...] = total


def cls_up_kernel(rows_ref, u0, u1, u2, d0, d1, d2, bias_ref, act_ref, slope_ref, sum_ref):
    tile = u0.shape[1]
    total = jnp.zeros(sum_ref.shape, F32)
    for p, (u, d) in enumerate(((u0, d0), (u1, d1), (u2, d2))):
        span = slice(p * tile, (p + 1) * tile)
        act, slope = gelu_pair(dot_nn(rows_ref[...], u[...]) + bias_ref[:, span])
        low = act.astype(BF)
        act_ref[:, span] = low[: act_ref.shape[0]]
        slope_ref[:, span] = slope
        total += dot_nt(low, d[...])
    sum_ref[...] = total


def cls_up_back_kernel(rows_ref, u0, u1, u2, d0, d1, d2, slope_ref, out_ref, sum_ref):
    tile = u0.shape[1]
    total = jnp.zeros(sum_ref.shape, F32)
    for p, (u, d) in enumerate(((u0, d0), (u1, d1), (u2, d2))):
        span = slice(p * tile, (p + 1) * tile)
        low = (dot_nn(rows_ref[...], d[...]) * slope_ref[:, span]).astype(BF)
        out_ref[:, span] = low[: out_ref.shape[0]]
        total += dot_nt(low, u[...])
    sum_ref[...] = total


def block_at(at, *_):
    return 0, at


def whole(array):
    return pl.BlockSpec(array.shape, lambda *_: (0,) * array.ndim)


def cls_call(kernel, name, count, before, weights, tile, after, outs):
    shapes = [jax.ShapeDtypeStruct(*o) for o in outs]
    dim = weights[0][0].shape[0]
    scalars = [] if count is None else [count]
    return pl.pallas_call(
        kernel,
        grid_spec=pltpu.PrefetchScalarGridSpec(
            num_scalar_prefetch=len(scalars),
            grid=(1,),
            in_specs=[whole(before)]
            + [pl.BlockSpec((dim, tile), functools.partial(block_at, at)) for _, at in weights]
            + [whole(after)],
            out_specs=[whole(o) for o in shapes],
        ),
        out_shape=shapes,
        cost_estimate=BRIEF,
        name=name,
    )(*scalars, before, *[w for w, _ in weights], after)


def owner_kernel(
    shape, two_ref, one_ref, pick_ref, uk, uf, dk, df, l0k, l0f, l1k, l1f, l2k, l2f,
    qkv_ref, out_ref, up_ref, down_ref, small_ref,
):
    width, hidden, dim, chunk, segments, scale_one, scale_two = shape
    rows = two_ref.shape[0]
    three = 3 * PAIR

    def put_kinds(block, values, add):
        for p in range(PIECES):
            for k in range(3):
                to = slice(k * width + p * PAIR, k * width + (p + 1) * PAIR)
                got = values[p][:, k * PAIR : (k + 1) * PAIR]
                qkv_ref[block, :, to] = qkv_ref[block, :, to] + got if add else got

    @pl.when(pl.program_id(0) == 0)
    def _():
        both = lambda a, b: (a[...].astype(F32) + b[...].astype(F32)) * scale_one
        up_ref[0] = both(uk, uf)
        down_ref[0] = both(dk, df)
        up_ref[1] = jnp.zeros_like(up_ref[1])
        down_ref[1] = jnp.zeros_like(down_ref[1])
        out_ref[1] = jnp.zeros_like(out_ref[1])
        qkv_ref[1] = jnp.zeros_like(qkv_ref[1])
        late = [both(a, b) for a, b in ((l0k, l0f), (l1k, l1f), (l2k, l2f))]
        put_kinds(0, late, False)
        for p in range(PIECES):
            out_ref[0, :, p * PAIR : (p + 1) * PAIR] = late[p][:, three : three + PAIR]
        small_ref[...] = l0k[:, three + PAIR :].astype(F32) + l0f[:, three + PAIR :].astype(F32)

    block = (lax.broadcasted_iota(jnp.int32, (rows, dim), 0) + rows * pl.program_id(0)) // segments
    col = lax.broadcasted_iota(jnp.int32, (rows, dim), 1)
    mine = (col >= block * chunk) & (col < block * chunk + chunk)

    def near(ref, at):
        picked = jnp.where(mine, ref[:, at : at + dim].astype(F32), 0.0).astype(BF)
        return dot_nn(picked, pick_ref[...]).astype(BF)

    at_pre, at_att, at_qkv = hidden, 2 * hidden, 2 * hidden + width
    at_two, at_one = at_qkv + 3 * width, at_qkv
    in_f, first_f, g_attn_f, g_mlp_f = (near(two_ref, at_two + k * dim) for k in range(4))
    first_1, g_mlp_1, g_attn_1 = (near(one_ref, at_one + k * dim) for k in range(3))
    up_ref[0] += dot_tn(first_1, one_ref[:, at_pre:at_att]) * scale_one
    down_ref[0] += dot_tn(g_mlp_1, one_ref[:, :at_pre]) * scale_one
    out_ref[0] += dot_tn(g_attn_1, one_ref[:, at_att:at_qkv]) * scale_one
    up_ref[1] += dot_tn(first_f, two_ref[:, at_pre:at_att]) * scale_two
    down_ref[1] += dot_tn(g_mlp_f, two_ref[:, :at_pre]) * scale_two
    out_ref[1] += dot_tn(g_attn_f, two_ref[:, at_att:at_qkv]) * scale_two
    grad = dot_tn(in_f, two_ref[:, at_qkv:at_two]) * scale_two
    put_kinds(1, [grad[:, p * three : (p + 1) * three] for p in range(PIECES)], True)


def owner_sums(shape, two, one, sums):
    width, hidden, dim, chunk, segments, _, _ = shape
    rows = min(128, two.shape[0])
    pick = jnp.asarray(np.tile(np.eye(chunk), (dim // chunk, 1)), BF)
    outs = [
        jax.ShapeDtypeStruct(o, F32)
        for o in ((2, chunk, 3 * width), (2, chunk, width), (2, chunk, hidden), (2, chunk, hidden), (chunk, PAIR))
    ]
    return pl.pallas_call(
        functools.partial(owner_kernel, shape),
        grid=(two.shape[0] // rows,),
        in_specs=[pl.BlockSpec((rows, m.shape[1]), lambda i: (i, 0)) for m in (two, one)]
        + [whole(m) for m in (pick, *sums)],
        out_specs=[whole(o) for o in outs],
        out_shape=outs,
        cost_estimate=BRIEF,
        name="owner_sums",
    )(two, one, pick, *sums)


def norm_stats(values):
    centred = values - jnp.mean(values, axis=-1, keepdims=True)
    inv = lax.rsqrt(jnp.mean(centred * centred, axis=-1, keepdims=True) + EPS_NORM)
    return centred * inv, inv


def norm_bwd(grad, unit, inv, gain):
    scaled = grad * gain
    along = jnp.mean(scaled * unit, axis=-1, keepdims=True)
    return inv * (scaled - jnp.mean(scaled, axis=-1, keepdims=True) - unit * along)


def column_sum(values):
    return jnp.sum(values, axis=0)


def advance(anchor, *moving):
    anchor = settle(anchor, *moving)
    going = [m for m in moving if m.left()]
    return launch(anchor, *going)


def local(
    layer_input,
    cotangent,
    lengths,
    w_qkv,
    w_out,
    w_up,
    w_down,
    vec_bias,
    norm_gain,
    bias_up,
    seg_pos,
):
    count = lax.axis_size("dp")
    bits = count.bit_length() - 1
    me = lax.axis_index("dp")
    part = lax.axis_index("tensor")
    seqs_here, half, dim = layer_input.shape
    full_len = 2 * half
    segments = full_len // SEG
    seg_half = half // SEG
    chunk = dim // count
    width = w_qkv.shape[3]
    hidden = w_up.shape[2]
    tile = hidden // PIECES
    three = 3 * PAIR
    orders = bit_orders(bits)
    swap_half = swap_tensor

    row_id = lax.broadcasted_iota(jnp.int32, (dim, dim), 0)
    col_id = lax.broadcasted_iota(jnp.int32, (dim, dim), 1)
    perm_hot = row_id == ((col_id // chunk) ^ me) * chunk + col_id % chunk
    perm = perm_hot.astype(BF)
    perm_f = perm_hot.astype(F32)

    def cut(matrix, size, p):
        return matrix[:, p * size : (p + 1) * size]

    def attn_piece(w_three, w_last, p):
        return jnp.concatenate([cut(w_three[:, k], PAIR, p) for k in range(3)] + [cut(w_last.T, PAIR, p)], axis=1)

    span = range(PIECES)
    one_q = Gather([attn_piece(w_qkv[0], w_out[0], p) for p in span], orders, bits, count)

    slot = me * 2 + part
    piece = vec_bias.shape[2]
    place = (
        lax.broadcasted_iota(jnp.int32, (piece, dim), 1)
        == lax.broadcasted_iota(jnp.int32, (piece, dim), 0) + slot * piece
    ).astype(F32)
    piece_up = bias_up.shape[1]
    hidden_all = piece_up * count * 2
    place_up = (
        lax.broadcasted_iota(jnp.int32, (piece_up, hidden_all), 1)
        == lax.broadcasted_iota(jnp.int32, (piece_up, hidden_all), 0) + slot * piece_up
    ).astype(F32)
    small_rows = jnp.concatenate(
        [vec_bias.reshape(-1, piece), norm_gain.reshape(-1, piece), seg_pos], axis=0
    )
    fold = hidden_all // dim
    small = jnp.concatenate(
        [dot_exact(small_rows, place), dot_exact(bias_up, place_up).reshape(2 * fold, dim)], axis=0
    )
    one_q.send()
    small = small + swap_tensor(small)
    for bit in range(bits - 2):
        small = small + swap_dp(small, bit, count)
    small = settle(small, one_q)
    small, w_qkv, w_out, w_up, w_down = tie(small, w_qkv, w_out, w_up, w_down)
    two_attn = jnp.concatenate([attn_piece(w_qkv[1], w_out[1], p) for p in span], axis=1)
    one_m = Gather([w_up[0], w_down[0].T, two_attn], orders[1:] + orders[:1], bits, count)
    two = Gather([w_up[1], w_down[1].T], orders[1:], bits, count)
    got = swap_dp(small, bits - 2, count)
    one_q.send()
    small = small + settle(got, one_q)
    small = launch(small, one_q)
    last = swap_dp(small, bits - 1, count)
    small = advance(small, one_q)
    while one_q.left() > 1:
        small = advance(small, one_q)
    small, *one_m.state = tie(small, *one_m.state)
    small = launch(small, one_m)
    small = small + last

    plain = small[: small_rows.shape[0]]
    up_all = small[small_rows.shape[0] :].reshape(2, 2, hidden)
    rel = dot_exact(plain, perm_f)

    def own_width(row):
        return jnp.where(part == 0, row[:width], row[width:])

    def block_vectors(block, order):
        base = 6 * block
        zero = jnp.zeros((PAIR,), F32)
        bias_q, bias_v = own_width(plain[base]), own_width(plain[base + 1])
        bias_qkv = jnp.concatenate(
            [v for p in span for v in (bias_q[p * PAIR : (p + 1) * PAIR], zero, bias_v[p * PAIR : (p + 1) * PAIR])]
        )
        gain_at = 12 + 2 * block
        return dict(
            qkv=bias_qkv,
            attn=order[base + 2],
            mlp=order[base + 3],
            shift_one=order[base + 4],
            shift_two=order[base + 5],
            gain_one=order[gain_at],
            gain_two=order[gain_at + 1],
            hidden=jnp.where(part == 0, up_all[block, 0], up_all[block, 1]),
        )

    v1, v2 = block_vectors(0, rel), block_vectors(1, rel)
    seg_rows = rel[16 : 16 + segments]

    length = lengths[0]
    seg_ids = jnp.concatenate(
        [part * seg_half + jnp.arange(seg_half), (1 - part) * seg_half + jnp.arange(seg_half)]
    ).astype(jnp.int32)
    seg_counts = jnp.clip(length - seg_ids * SEG, 0, SEG).astype(jnp.int32)
    cls_count = ((lengths + (SEG - 1)) // SEG).astype(jnp.int32)

    pad_rows = -segments % 16

    def padded(rows):
        return jnp.concatenate([rows, jnp.zeros((pad_rows, rows.shape[1]), rows.dtype)], axis=0)

    def turned(rows):
        return jnp.where(part == 0, rows, jnp.concatenate([rows[seg_half:], rows[:seg_half]], axis=0))

    def both_halves(own_rows):
        return turned(jnp.concatenate([own_rows, swap_half(own_rows)], axis=0))

    def own_half(rows):
        return jnp.where(part == 0, rows[:seg_half], rows[seg_half:segments])

    def firsts(rows):
        return rows.reshape(-1, SEG, rows.shape[-1])[:, 0]

    x_own = dot_nn(layer_input[0], perm).astype(BF)
    x_full = jnp.concatenate([x_own, swap_half(x_own)], axis=0)
    x_full = settle(x_full, one_q)
    attn_r = one_q.results()
    w_qkv_r = jnp.concatenate([w[:, :three] for w in attn_r], axis=1)
    w_out_r = jnp.concatenate([w[:, three:] for w in attn_r], axis=1)
    qkv = (dot_nn(x_full, w_qkv_r) + v1["qkv"]).astype(BF)
    qkv = advance(qkv, one_m)
    attended = attn_fwd(seg_counts, qkv)
    while one_m.left() > 2:
        attended = advance(attended, one_m)
    attended, *two.state = tie(attended, *two.state)
    attended = launch(attended, two)
    partial_attn = dot_nt(attended, w_out_r).astype(BF)
    first_sum = (
        partial_attn[:half].astype(F32)
        + swap_half(partial_attn[half:]).astype(F32)
        + v1["attn"]
        + x_own.astype(F32)
    )
    unit_one, inv_one = norm_stats(first_sum)
    first = unit_one * v1["gain_one"] + v1["shift_one"]
    first_low = first.astype(BF)
    first_full = jnp.concatenate([first_low, swap_half(first_low)], axis=0)
    first_full = settle(first_full, one_m, two)
    first_full = launch(first_full, one_m)
    first_full = launch(first_full, two)
    first_full = settle(first_full, one_m)
    w_up_r, w_down_r, two_attn_r = one_m.results()
    act, slope = up_gelu(first_full, w_up_r, v1["hidden"])
    while two.left() > 3:
        act = advance(act, two)
    act = advance(act, two)
    partial_mlp = dot_nt(act, w_down_r).astype(BF)
    second_sum = (
        partial_mlp[:half].astype(F32) + swap_half(partial_mlp[half:]).astype(F32) + v1["mlp"] + first
    )
    while two.left() > 1:
        second_sum = advance(second_sum, two)
    unit_two, inv_two = norm_stats(second_sum)
    first_out = unit_two * v1["gain_two"] + v1["shift_two"]

    row_in = lax.broadcasted_iota(jnp.int32, (half, 1), 0)
    valid = part * half + row_in < length
    is_cls = lax.broadcasted_iota(jnp.int32, (1, SEG, 1), 1) == 0

    def with_cls(rows, cls):
        return jnp.where(is_cls, cls[:, None, :], rows.reshape(seg_half, SEG, dim)).reshape(half, dim)

    cot = jnp.where(valid, cotangent[0], jnp.zeros_like(cotangent[0]))
    grad_y_low = dot_nn(cot, perm).astype(BF)
    grad_out = with_cls(grad_y_low.astype(F32), jnp.zeros((seg_half, dim), F32))
    g_second = norm_bwd(grad_out, unit_two, inv_two, v1["gain_two"])
    g_second_low = g_second.astype(BF)
    g_mlp = jnp.concatenate([g_second_low, swap_half(g_second_low)], axis=0)
    gpre = (dot_nn(g_mlp, w_down_r) * slope.astype(F32)).astype(BF)
    part_h = dot_nt(gpre, w_up_r).astype(BF)
    gw_up = dot_tn(first_full, gpre).astype(BF)
    gw_down = dot_tn(g_mlp, act).astype(BF)
    g_first = part_h[:half].astype(F32) + swap_half(part_h[half:]).astype(F32) + g_second
    g_first_sum = norm_bwd(g_first, unit_one, inv_one, v1["gain_one"])
    g_first_low = g_first_sum.astype(BF)
    g_attn = jnp.concatenate([g_first_low, swap_half(g_first_low)], axis=0)
    g_attended = dot_nn(g_attn, w_out_r).astype(BF)
    gw_out = dot_tn(g_attn, attended).astype(BF)
    early = Scatter([[gw_up], [gw_down]], orders[1:], bits, count)
    g_attended = launch(g_attended, early)

    sums_own = jnp.concatenate([firsts(second_sum), firsts(first_sum)], axis=0)
    sums_other = swap_half(sums_own)
    second_sum_1 = padded(turned(jnp.concatenate([sums_own[:seg_half], sums_other[:seg_half]], axis=0)))
    first_sum_1 = padded(turned(jnp.concatenate([sums_own[seg_half:], sums_other[seg_half:]], axis=0)))
    unit_two_1, inv_two_1 = norm_stats(second_sum_1)
    unit_one_1, inv_one_1 = norm_stats(first_sum_1)
    first_low_1 = (unit_one_1 * v1["gain_one"] + v1["shift_one"]).astype(BF)
    act_1, slope_1, att_1 = (turned(firsts(v)) for v in (act, slope, attended))
    cls_rel = unit_two_1 * v1["gain_two"] + v1["shift_two"]
    cls_in = padded(cls_rel[:segments] + seg_rows)
    g_c = padded(both_halves(firsts(grad_y_low))).astype(F32)

    cls_in, g_attended, gw_out = tie(cls_in, g_attended, gw_out)
    cls_in = settle(cls_in, two)
    attn_w = [(two_attn_r, p) for p in span]
    up_w, down_w = ([(w, p) for p in span] for w in two.results())
    cls_low = cls_in.astype(BF)
    rows_c = cls_in.shape[0]
    qkv_c, att_c, part_c = cls_call(
        cls_attn_kernel, "cls_attn", cls_count, cls_low, attn_w, tile, v2["qkv"][None, :],
        [((rows_c, 3 * width), BF), ((segments, width), BF), ((rows_c, dim), F32)],
    )
    sum_c1 = part_c + swap_half(part_c) + v2["attn"] + cls_in
    unit_c1, inv_c1 = norm_stats(sum_c1)
    first_c = unit_c1 * v2["gain_one"] + v2["shift_one"]
    first_c_low = first_c.astype(BF)
    act_c, slope_c, part_c2 = cls_call(
        cls_up_kernel, "cls_up", None, first_c_low, up_w + down_w, tile, v2["hidden"][None, :],
        [((segments, hidden), BF), ((rows_c, hidden), F32), ((rows_c, dim), F32)],
    )
    sum_c2 = part_c2 + swap_half(part_c2) + v2["mlp"] + first_c
    unit_c2, inv_c2 = norm_stats(sum_c2)
    cls_out = unit_c2 * v2["gain_two"] + v2["shift_two"]
    combined = jnp.where(valid, with_cls(first_out, own_half(cls_out)), 0.0).astype(BF)
    output = dot_nn(combined, perm).astype(BF)[None]

    g_second_c = norm_bwd(g_c, unit_c2, inv_c2, v2["gain_two"])
    g_mlp_c = g_second_c.astype(BF)
    back_outs = [((segments, hidden), BF), ((rows_c, dim), F32)]
    gpre_c, part_g1 = cls_call(
        cls_up_back_kernel, "cls_up_back", None, g_mlp_c, up_w + down_w, tile, slope_c, back_outs
    )
    g_first_c = part_g1 + swap_half(part_g1) + g_second_c
    g_sum_c = norm_bwd(g_first_c, unit_c1, inv_c1, v2["gain_one"])
    g_attn_c = g_sum_c.astype(BF)
    gqkv_c, part_g2 = cls_call(
        cls_attn_back_kernel, "cls_attn_back", cls_count, g_attn_c, attn_w, tile, qkv_c,
        [((segments, 3 * width), BF), ((rows_c, dim), F32)],
    )
    g_cls_in = part_g2 + swap_half(part_g2) + g_sum_c
    near_two = tuple(f[:segments] for f in (cls_low, first_c_low, g_attn_c, g_mlp_c))
    far_two = (act_c, gpre_c, att_c, gqkv_c) + near_two
    wide_two = Gather([jnp.concatenate(far_two, axis=1)], orders[:1], bits, count)
    while early.left() > 3:
        g_cls_in = advance(g_cls_in, early)
    g_cls_in = launch(g_cls_in, wide_two)

    g_second_1 = norm_bwd(g_cls_in, unit_two_1, inv_two_1, v1["gain_two"])
    g_mlp_1 = g_second_1.astype(BF)
    gpre_1, part_1 = cls_call(
        cls_up_back_kernel, "cls_up_back", None, g_mlp_1, [(w, p) for w in (w_up_r, w_down_r) for p in span], tile,
        padded(slope_1.astype(F32)), back_outs
    )
    g_first_1 = part_1 + swap_half(part_1) + g_second_1
    g_sum_1 = norm_bwd(g_first_1, unit_one_1, inv_one_1, v1["gain_one"])
    g_attn_1 = g_sum_1.astype(BF)
    g_att_1 = turned(dot_nn(g_attn_1, w_out_r).astype(BF)[:segments])

    near_one = tuple(f[:segments] for f in (first_low_1, g_mlp_1, g_attn_1))
    far_one = (act_1, gpre_1, att_1) + near_one
    wide_one = Gather([jnp.concatenate(far_one, axis=1)], orders[1:2], bits, count)
    g_att_1 = advance(g_att_1, early, wide_two)
    g_att_1 = launch(g_att_1, wide_one)

    scale_one = 1.0 / math.sqrt(seqs_here * count * full_len)
    scale_two = 1.0 / math.sqrt(seqs_here * count * segments)

    def spread(values, total):
        zero = jnp.zeros((total - values.shape[0],), F32)
        return jnp.where(part == 0, jnp.concatenate([values, zero]), jnp.concatenate([zero, values]))

    def both_sums(rows, cls):
        return (column_sum(rows) + column_sum(own_half(cls))) * scale_one

    def cls_sums(cls):
        return column_sum(own_half(cls)) * scale_two

    sums_c = column_sum(gqkv_c.astype(F32)).reshape(PIECES, 3, PAIR) * scale_two
    rel_rows = jnp.stack(
        [
            both_sums(g_first_sum, g_sum_1),
            both_sums(g_second, g_second_1),
            both_sums(g_first, g_first_1),
            both_sums(grad_out, g_cls_in),
            cls_sums(g_sum_c),
            cls_sums(g_second_c),
            cls_sums(g_first_c),
            cls_sums(g_c),
            both_sums(g_first * unit_one, g_first_1 * unit_one_1),
            both_sums(grad_out * unit_two, g_cls_in * unit_two_1),
            cls_sums(g_first_c * unit_c1),
            cls_sums(g_c * unit_c2),
        ]
    )
    zeros_half = jnp.zeros((seg_half, dim), F32)
    cls_part = own_half(g_cls_in) * scale_two
    seg_grad = jnp.where(
        part == 0,
        jnp.concatenate([cls_part, zeros_half], axis=0),
        jnp.concatenate([zeros_half, cls_part], axis=0),
    )
    up_rows = jnp.stack(
        [
            spread((dot_nn(jnp.ones((16, 2 * half), BF), gpre)[0] + column_sum(gpre_1.astype(F32))) * scale_one, hidden_all),
            spread(column_sum(gpre_c.astype(F32)) * scale_two, hidden_all),
        ]
    )
    per_row = 2 * hidden_all // dim
    by_owner = up_rows.reshape(2, count, -1).transpose(1, 0, 2).reshape(dim, per_row)
    plain_rows = jnp.stack([spread(sums_c[:, k].reshape(-1), dim) for k in (0, 2)])
    canon = dot_exact(jnp.concatenate([plain_rows, by_owner.T], axis=0), perm_f)
    small_rows = jnp.concatenate([rel_rows, seg_grad, canon], axis=0)
    small_rows = small_rows + swap_tensor(small_rows)
    filler = jnp.zeros((PAIR - small_rows.shape[0] - 2, dim), F32)
    small_cols = jnp.concatenate([small_rows, filler], axis=0).T.astype(BF)
    g_att_1, small_cols = tie(g_att_1, small_cols)

    gqkv, gqkv_sums = attn_bwd(seg_counts, qkv, g_attended, g_att_1)
    gqkv = advance(gqkv, early, wide_two, wide_one)
    gw_qkv = dot_tn(x_full, gqkv).astype(BF)
    sums_o = gqkv_sums.reshape(PIECES, 3, PAIR) * scale_one
    bias_own = jnp.stack([spread(sums_o[:, k].reshape(-1), dim) for k in (0, 2)])
    bias_cols = dot_exact(bias_own + swap_tensor(bias_own), perm_f).T.astype(BF)
    small_cols = jnp.concatenate([small_cols, bias_cols], axis=1)
    late = Scatter(
        [[cut(gw_qkv, three, p), cut(gw_out, PAIR, p)] + [small_cols] * (p == 0) for p in span], orders, bits, count
    )
    gqkv = launch(gqkv, late)
    wides = (wide_two, wide_one)
    gqkv = advance(gqkv, *wides)
    part_x = dot_nt(gqkv, w_qkv_r).astype(BF)

    part_x = advance(part_x, late)
    g_first_all = with_cls(g_first_sum, own_half(g_sum_1))
    g_in = part_x[:half].astype(F32) + swap_half(part_x[half:]).astype(F32) + g_first_all
    g_in_high = lax.reduce_precision(g_in, 8, 7)
    grad_input = (dot_nn(g_in_high.astype(BF), perm) + dot_nn((g_in - g_in_high).astype(BF), perm))[None]
    anchor = jnp.zeros((), F32)
    while any(m.left() > 1 for m in (early, *wides)):
        anchor = advance(anchor, *[m for m in (early, *wides) if m.left() > 1])
    while late.left() > 1:
        anchor = advance(anchor, late)
    anchor = settle(anchor, late, early, *wides)

    shape = (width, hidden, dim, chunk, segments, scale_one, scale_two)
    grad_three, grad_last, grad_w_up, grad_down, small_own = owner_sums(
        shape, wide_two.results()[0], wide_one.results()[0], early.pairs() + late.pairs()
    )
    grad_w_qkv = grad_three.reshape(2, chunk, 3, width)
    grad_w_out = grad_last.transpose(0, 2, 1)
    grad_w_down = grad_down.transpose(0, 2, 1)

    mine = small_own.T
    rows_own = jnp.where(part == 0, mine[:, :piece], mine[:, piece:])
    vecs = rows_own[:12]
    grad_vec = jnp.concatenate([rows_own[PAIR - 2 :], vecs[:4], rows_own[20:22], vecs[4:8]], axis=0).reshape(2, 6, piece)
    grad_gain = vecs[8:].reshape(2, 2, piece)
    grad_seg = rows_own[12:20]
    up_own = mine[22 : 22 + per_row].T.reshape(2, 2, piece_up)
    grad_up_vec = jnp.where(part == 0, up_own[:, 0], up_own[:, 1])
    return (
        output,
        grad_input,
        grad_w_qkv,
        grad_w_out,
        grad_w_up,
        grad_w_down,
        grad_vec,
        grad_gain,
        grad_up_vec,
        grad_seg,
    )


def solution(mesh):
    return jax.shard_map(
        local,
        mesh=mesh,
        in_specs=(
            P("dp", "tensor", None),
            P("dp", "tensor", None),
            P("dp"),
            P(None, "dp", None, "tensor"),
            P(None, "tensor", "dp"),
            P(None, "dp", "tensor"),
            P(None, "tensor", "dp"),
            P(None, None, ("dp", "tensor")),
            P(None, None, ("dp", "tensor")),
            P(None, ("dp", "tensor")),
            P(None, ("dp", "tensor")),
        ),
        out_specs=(
            P("dp", "tensor", None),
            P("dp", "tensor", None),
            P(None, "dp", None, "tensor"),
            P(None, "tensor", "dp"),
            P(None, "dp", "tensor"),
            P(None, "tensor", "dp"),
            P(None, None, ("dp", "tensor")),
            P(None, None, ("dp", "tensor")),
            P(None, ("dp", "tensor")),
            P(None, ("dp", "tensor")),
        ),
        check_vma=False,
    )
```

```python
import functools
import math

import jax
import jax.numpy as jnp
import numpy as np
from jax import lax
from jax.experimental import pallas as pl
from jax.experimental.pallas import tpu as pltpu
from jax.sharding import PartitionSpec as P

HD = 64
SEG = 128
NEG_FILL = -1000000000.0
EPS_NORM = 1e-06
BF = jnp.bfloat16
F32 = jnp.float32
INV_SQRT2 = 1.0 / math.sqrt(2.0)
INV_SQRT2PI = 1.0 / math.sqrt(2.0 * math.pi)
SM_SCALE = HD ** (-0.5)
PAIR = 2 * HD
PIECES = 3
BRIEF = pl.CostEstimate(flops=1, bytes_accessed=1, transcendentals=0)


def dot_nn(a, b):
    return lax.dot_general(a, b, (((1,), (0,)), ((), ())), preferred_element_type=F32)


def dot_nt(a, b):
    return lax.dot_general(a, b, (((1,), (1,)), ((), ())), preferred_element_type=F32)


def dot_tn(a, b):
    return lax.dot_general(a, b, (((0,), (0,)), ((), ())), preferred_element_type=F32)


def dot_exact(a, b):
    return lax.dot_general(
        a, b, (((1,), (0,)), ((), ())), precision=lax.Precision.HIGHEST, preferred_element_type=F32
    )


def swap_dp(values, bit, count):
    return lax.ppermute(values, "dp", [(i, i ^ (1 << bit)) for i in range(count)])


def swap_tensor(values):
    return lax.ppermute(values, "tensor", [(0, 1), (1, 0)])


def bit_orders(bits):
    if bits == 4:
        return ((3, 2, 0, 1), (3, 1, 2, 0), (3, 0, 1, 2))
    base = tuple(range(bits))
    return (base, base[1:] + base[:1], base[2:] + base[:2])


def tie(*values):
    return lax.optimization_barrier(values)


def join(low, high, bit, bits):
    return jnp.concatenate([low, high], axis=bits - 1 - bit)


class Gather:
    def __init__(self, pieces, orders, bits, count):
        self.state = [u.reshape((1,) * bits + u.shape) for u in pieces]
        self.orders, self.bits, self.count, self.step = orders, bits, count, 0

    def send(self):
        self.flying = [
            swap_dp(v, self.orders[i][self.step], self.count) for i, v in enumerate(self.state)
        ]

    def land(self):
        self.state = [
            join(v, f, self.orders[i][self.step], self.bits)
            for i, (v, f) in enumerate(zip(self.state, self.flying))
        ]
        self.step += 1

    def left(self):
        return self.bits - self.step

    def results(self):
        return [v.reshape((-1, v.shape[-1])) for v in self.state]


def half_of(values, axis, index):
    return lax.index_in_dim(values, index, axis, keepdims=True)


class Scatter:
    def __init__(self, pieces, orders, bits, count):
        self.bits, self.count, self.step = bits, count, 0
        self.orders = [tuple(reversed(o)) for o in orders]
        self.parts = [[[m.reshape((2,) * bits + (-1, m.shape[-1])) for m in piece]] for piece in pieces]

    def half(self, which, index):
        axis = self.bits - 1 - self.orders[which][self.step]
        cut = [
            jnp.concatenate([half_of(m, axis, index) for m in part], axis=-1).astype(F32)
            for part in self.parts[which]
        ]
        return sum(cut[1:], cut[0]).astype(BF)

    def prepare(self):
        self.leaving = [self.half(i, 1) for i in range(len(self.parts))]

    def send(self):
        self.flying = [
            swap_dp(v, self.orders[i][self.step], self.count) for i, v in enumerate(self.leaving)
        ]
        self.kept = [self.half(i, 0) for i in range(len(self.parts))]

    def land(self):
        self.parts = [[[k], [f]] for k, f in zip(self.kept, self.flying)]
        self.step += 1

    def left(self):
        return self.bits - self.step

    def pairs(self):
        return [side[0].reshape((-1, side[0].shape[-1])) for part in self.parts for side in part]


def settle(anchor, *moving):
    flat = [f for m in moving for f in m.flying]
    anchor, *flat = tie(anchor, *flat)
    for m in moving:
        m.flying = flat[: len(m.flying)]
        flat = flat[len(m.flying) :]
        m.land()
    return anchor


def launch(anchor, *moving):
    for m in moving:
        if isinstance(m, Scatter):
            m.prepare()
            anchor, *m.leaving = tie(anchor, *m.leaving)
        elif isinstance(m, Gather):
            anchor, *m.state = tie(anchor, *m.state)
        else:
            anchor, m.state = tie(anchor, m.state)
        m.send()
    return anchor


def pair_masks(rows):
    lane = lax.broadcasted_iota(jnp.int32, (rows, PAIR), 1)
    return lane < HD


def stack_heads(two, low_half):
    zero = jnp.zeros_like(two)
    return jnp.concatenate([jnp.where(low_half, two, zero), jnp.where(low_half, zero, two)], axis=0)


def merge_heads(stacked, low_half, rows):
    return jnp.where(low_half, stacked[:rows], stacked[rows:])


def pair_probs(q_stack, key_two, allowed):
    scores = dot_nt(q_stack, key_two) * SM_SCALE
    scores = jnp.where(allowed, scores, NEG_FILL)
    expo = jnp.exp(scores - jnp.max(scores, axis=-1, keepdims=True))
    return expo * (1.0 / jnp.sum(expo, axis=-1, keepdims=True))


def row_window(rows):
    return [pl.BlockSpec((SEG, cols), lambda i, c: (i, 0)) for cols in rows]


def attn_fwd_kernel(count_ref, qkv_ref, out_ref):
    rows = qkv_ref.shape[0]
    low_half = pair_masks(rows)
    allowed = lax.broadcasted_iota(jnp.int32, (2 * rows, rows), 1) < count_ref[pl.program_id(0)]
    for pair in range(out_ref.shape[1] // PAIR):
        at = 3 * pair * PAIR
        q_stack = stack_heads(qkv_ref[:, at : at + PAIR], low_half)
        probs = pair_probs(q_stack, qkv_ref[:, at + PAIR : at + 2 * PAIR], allowed)
        mixed = dot_nn(probs.astype(BF), qkv_ref[:, at + 2 * PAIR : at + 3 * PAIR])
        out_ref[:, pair * PAIR : (pair + 1) * PAIR] = merge_heads(mixed, low_half, rows).astype(BF)


def pair_bwd(qkv, grad, allowed, low_half):
    rows = grad.shape[0]
    key_two = qkv[:, PAIR : 2 * PAIR]
    q_stack = stack_heads(qkv[:, :PAIR], low_half)
    g_stack = stack_heads(grad, low_half)
    probs = pair_probs(q_stack, key_two, allowed)
    grad_probs = dot_nt(g_stack, qkv[:, 2 * PAIR :])
    inner = jnp.sum(grad_probs * probs, axis=-1, keepdims=True)
    grad_scores = jnp.where(allowed, probs * (grad_probs - inner), 0.0).astype(BF)
    return (
        merge_heads(dot_nn(grad_scores, key_two), low_half, rows) * SM_SCALE,
        dot_tn(grad_scores, q_stack) * SM_SCALE,
        dot_tn(probs.astype(BF), g_stack),
    )


def attn_bwd_kernel(count_ref, qkv_ref, grad_ref, first_ref, out_ref, sums_ref):
    rows = qkv_ref.shape[0]
    low_half = pair_masks(rows)
    allowed = lax.broadcasted_iota(jnp.int32, (2 * rows, rows), 1) < count_ref[pl.program_id(0)]
    is_first = lax.broadcasted_iota(jnp.int32, (rows, PAIR), 0) == 0

    @pl.when(pl.program_id(0) == 0)
    def _():
        sums_ref[...] = jnp.zeros_like(sums_ref)

    for pair in range(grad_ref.shape[1] // PAIR):
        at = 3 * pair * PAIR
        span = slice(pair * PAIR, (pair + 1) * PAIR)
        grad = jnp.where(is_first, first_ref[0, :, span], grad_ref[:, span].astype(F32)).astype(BF)
        for k, values in enumerate(pair_bwd(qkv_ref[:, at : at + 3 * PAIR], grad, allowed, low_half)):
            low = values.astype(BF)
            to = slice(at + k * PAIR, at + (k + 1) * PAIR)
            out_ref[:, to] = low
            sums_ref[:, to] += jnp.sum(low.astype(F32), axis=0, keepdims=True)


def attn_fwd(counts, qkv):
    rows, three = qkv.shape
    width = three // 3
    return pl.pallas_call(
        attn_fwd_kernel,
        grid_spec=pltpu.PrefetchScalarGridSpec(
            num_scalar_prefetch=1,
            grid=(rows // SEG,),
            in_specs=row_window([three]),
            out_specs=row_window([width])[0],
        ),
        out_shape=jax.ShapeDtypeStruct((rows, width), BF),
        cost_estimate=BRIEF,
        name="attn_fwd",
    )(counts, qkv)


def attn_bwd(counts, qkv, grad, grad_first):
    rows, three = qkv.shape
    width = three // 3
    return pl.pallas_call(
        attn_bwd_kernel,
        grid_spec=pltpu.PrefetchScalarGridSpec(
            num_scalar_prefetch=1,
            grid=(rows // SEG,),
            in_specs=row_window([three, width]) + [pl.BlockSpec((1, 1, width), lambda i, c: (i, 0, 0))],
            out_specs=row_window([three]) + [pl.BlockSpec((1, three), lambda i, c: (0, 0))],
        ),
        out_shape=[jax.ShapeDtypeStruct((rows, three), BF), jax.ShapeDtypeStruct((1, three), F32)],
        cost_estimate=BRIEF,
        name="attn_bwd",
    )(counts, qkv, grad, grad_first.astype(F32)[:, None, :])


def gelu_pair(pre):
    cdf = 0.5 * (1.0 + lax.erf(pre * INV_SQRT2))
    return pre * cdf, cdf + pre * (jnp.exp(-0.5 * pre * pre) * INV_SQRT2PI)


def up_kernel(rows_ref, w_ref, bias_ref, act_ref, slope_ref):
    act, slope = gelu_pair(dot_nn(rows_ref[...], w_ref[...]) + bias_ref[...])
    act_ref[...] = act.astype(BF)
    slope_ref[...] = slope.astype(BF)


def up_gelu(rows, w_up, bias):
    total, dim = rows.shape
    hidden = w_up.shape[1]
    tile_r = min(256, total)
    tile_h = min(512, hidden)
    spec_out = pl.BlockSpec((tile_r, tile_h), lambda j, i: (i, j))
    return pl.pallas_call(
        up_kernel,
        grid=(hidden // tile_h, total // tile_r),
        in_specs=[
            pl.BlockSpec((tile_r, dim), lambda j, i: (i, 0)),
            pl.BlockSpec((dim, tile_h), lambda j, i: (0, j)),
            pl.BlockSpec((1, tile_h), lambda j, i: (0, j)),
        ],
        out_specs=[spec_out, spec_out],
        out_shape=[jax.ShapeDtypeStruct((total, hidden), BF)] * 2,
        cost_estimate=BRIEF,
        name="up_gelu",
    )(rows, w_up, bias)


def cls_attn_kernel(count_ref, rows_ref, w0, w1, w2, bias_ref, qkv_ref, att_ref, sum_ref):
    rows = rows_ref.shape[0]
    low_half = pair_masks(rows)
    allowed = lax.broadcasted_iota(jnp.int32, (2 * rows, rows), 1) < count_ref[0]
    total = jnp.zeros(sum_ref.shape, F32)
    for p, w in enumerate((w0, w1, w2)):
        span = slice(3 * p * PAIR, 3 * (p + 1) * PAIR)
        qkv = (dot_nn(rows_ref[...], w[:, : 3 * PAIR]) + bias_ref[:, span]).astype(BF)
        qkv_ref[:, span] = qkv
        probs = pair_probs(stack_heads(qkv[:, :PAIR], low_half), qkv[:, PAIR : 2 * PAIR], allowed)
        att = merge_heads(dot_nn(probs.astype(BF), qkv[:, 2 * PAIR :]), low_half, rows).astype(BF)
        att_ref[:, p * PAIR : (p + 1) * PAIR] = att[: att_ref.shape[0]]
        total += dot_nt(att, w[:, 3 * PAIR :])
    sum_ref[...] = total


def cls_attn_back_kernel(count_ref, grad_ref, w0, w1, w2, qkv_ref, out_ref, sum_ref):
    rows = grad_ref.shape[0]
    low_half = pair_masks(rows)
    allowed = lax.broadcasted_iota(jnp.int32, (2 * rows, rows), 1) < count_ref[0]
    total = jnp.zeros(sum_ref.shape, F32)
    for p, w in enumerate((w0, w1, w2)):
        span = slice(3 * p * PAIR, 3 * (p + 1) * PAIR)
        grad = dot_nn(grad_ref[...], w[:, 3 * PAIR :]).astype(BF)
        low = jnp.concatenate(pair_bwd(qkv_ref[:, span], grad, allowed, low_half), axis=1).astype(BF)
        out_ref[:, span] = low[: out_ref.shape[0]]
        total += dot_nt(low, w[:, : 3 * PAIR])
    sum_ref[...] = total


def cls_up_kernel(rows_ref, u0, u1, u2, d0, d1, d2, bias_ref, act_ref, slope_ref, sum_ref):
    tile = u0.shape[1]
    total = jnp.zeros(sum_ref.shape, F32)
    for p, (u, d) in enumerate(((u0, d0), (u1, d1), (u2, d2))):
        span = slice(p * tile, (p + 1) * tile)
        act, slope = gelu_pair(dot_nn(rows_ref[...], u[...]) + bias_ref[:, span])
        low = act.astype(BF)
        act_ref[:, span] = low[: act_ref.shape[0]]
        slope_ref[:, span] = slope
        total += dot_nt(low, d[...])
    sum_ref[...] = total


def cls_up_back_kernel(rows_ref, u0, u1, u2, d0, d1, d2, slope_ref, out_ref, sum_ref):
    tile = u0.shape[1]
    total = jnp.zeros(sum_ref.shape, F32)
    for p, (u, d) in enumerate(((u0, d0), (u1, d1), (u2, d2))):
        span = slice(p * tile, (p + 1) * tile)
        low = (dot_nn(rows_ref[...], d[...]) * slope_ref[:, span]).astype(BF)
        out_ref[:, span] = low[: out_ref.shape[0]]
        total += dot_nt(low, u[...])
    sum_ref[...] = total


def block_at(at, *_):
    return 0, at


def whole(array):
    return pl.BlockSpec(array.shape, lambda *_: (0,) * array.ndim)


def cls_call(kernel, name, count, before, weights, tile, after, outs):
    shapes = [jax.ShapeDtypeStruct(*o) for o in outs]
    dim = weights[0][0].shape[0]
    scalars = [] if count is None else [count]
    return pl.pallas_call(
        kernel,
        grid_spec=pltpu.PrefetchScalarGridSpec(
            num_scalar_prefetch=len(scalars),
            grid=(1,),
            in_specs=[whole(before)]
            + [pl.BlockSpec((dim, tile), functools.partial(block_at, at)) for _, at in weights]
            + [whole(after)],
            out_specs=[whole(o) for o in shapes],
        ),
        out_shape=shapes,
        cost_estimate=BRIEF,
        name=name,
    )(*scalars, before, *[w for w, _ in weights], after)


def own_bias_kernel(part_ref, rows_ref, qkv_ref, hidden_ref):
    width = rows_ref.shape[1] // 2
    first = part_ref[0] == 0
    fold = (rows_ref.shape[0] - 24) // 2

    def own(row, at, size):
        return jnp.where(first, rows_ref[row : row + 1, at : at + size], rows_ref[row : row + 1, width + at : width + at + size])

    for block in range(2):
        for p in range(PIECES):
            parts = (own(6 * block, p * PAIR, PAIR), jnp.zeros((1, PAIR), F32), own(6 * block + 1, p * PAIR, PAIR))
            for k, value in enumerate(parts):
                at = (3 * p + k) * PAIR
                qkv_ref[block : block + 1, at : at + PAIR] = value
        base = 24 + fold * block
        for k in range(fold // 2):
            low, high = base + k, base + fold // 2 + k
            value = jnp.where(first, rows_ref[low : low + 1, :], rows_ref[high : high + 1, :])
            hidden_ref[block : block + 1, 2 * width * k : 2 * width * (k + 1)] = value


def own_biases(part, rows, width, hidden):
    outs = [jax.ShapeDtypeStruct((2, 3 * width), F32), jax.ShapeDtypeStruct((2, hidden), F32)]
    return pl.pallas_call(
        own_bias_kernel,
        grid_spec=pltpu.PrefetchScalarGridSpec(
            num_scalar_prefetch=1,
            grid=(1,),
            in_specs=[whole(rows)],
            out_specs=[whole(o) for o in outs],
        ),
        out_shape=outs,
        cost_estimate=BRIEF,
        name="own_biases",
    )(part.reshape(1).astype(jnp.int32), rows)


def owner_kernel(
    shape, two_ref, one_ref, pick_ref, uk, uf, dk, df, l0k, l0f, l1k, l1f, l2k, l2f,
    qkv_ref, out_ref, up_ref, down_ref, small_ref,
):
    width, hidden, dim, chunk, segments, scale_one, scale_two = shape
    rows = two_ref.shape[0]
    three = 3 * PAIR

    def put_kinds(block, values, add):
        for p in range(PIECES):
            for k in range(3):
                to = slice(k * width + p * PAIR, k * width + (p + 1) * PAIR)
                got = values[p][:, k * PAIR : (k + 1) * PAIR]
                qkv_ref[block, :, to] = qkv_ref[block, :, to] + got if add else got

    @pl.when(pl.program_id(0) == 0)
    def _():
        both = lambda a, b: (a[...].astype(F32) + b[...].astype(F32)) * scale_one
        up_ref[0] = both(uk, uf)
        down_ref[0] = both(dk, df)
        up_ref[1] = jnp.zeros_like(up_ref[1])
        down_ref[1] = jnp.zeros_like(down_ref[1])
        out_ref[1] = jnp.zeros_like(out_ref[1])
        qkv_ref[1] = jnp.zeros_like(qkv_ref[1])
        late = [both(a, b) for a, b in ((l0k, l0f), (l1k, l1f), (l2k, l2f))]
        put_kinds(0, late, False)
        for p in range(PIECES):
            out_ref[0, :, p * PAIR : (p + 1) * PAIR] = late[p][:, three : three + PAIR]
        small_ref[...] = l0k[:, three + PAIR :].astype(F32) + l0f[:, three + PAIR :].astype(F32)

    block = (lax.broadcasted_iota(jnp.int32, (rows, dim), 0) + rows * pl.program_id(0)) // segments
    col = lax.broadcasted_iota(jnp.int32, (rows, dim), 1)
    mine = (col >= block * chunk) & (col < block * chunk + chunk)

    def near(ref, at):
        picked = jnp.where(mine, ref[:, at : at + dim].astype(F32), 0.0).astype(BF)
        return dot_nn(picked, pick_ref[...]).astype(BF)

    at_pre, at_att, at_qkv = hidden, 2 * hidden, 2 * hidden + width
    at_two, at_one = at_qkv + 3 * width, at_qkv
    in_f, first_f, g_attn_f, g_mlp_f = (near(two_ref, at_two + k * dim) for k in range(4))
    first_1, g_mlp_1, g_attn_1 = (near(one_ref, at_one + k * dim) for k in range(3))
    up_ref[0] += dot_tn(first_1, one_ref[:, at_pre:at_att]) * scale_one
    down_ref[0] += dot_tn(g_mlp_1, one_ref[:, :at_pre]) * scale_one
    out_ref[0] += dot_tn(g_attn_1, one_ref[:, at_att:at_qkv]) * scale_one
    up_ref[1] += dot_tn(first_f, two_ref[:, at_pre:at_att]) * scale_two
    down_ref[1] += dot_tn(g_mlp_f, two_ref[:, :at_pre]) * scale_two
    out_ref[1] += dot_tn(g_attn_f, two_ref[:, at_att:at_qkv]) * scale_two
    grad = dot_tn(in_f, two_ref[:, at_qkv:at_two]) * scale_two
    put_kinds(1, [grad[:, p * three : (p + 1) * three] for p in range(PIECES)], True)


def owner_sums(shape, two, one, sums):
    width, hidden, dim, chunk, segments, _, _ = shape
    rows = min(128, two.shape[0])
    pick = jnp.asarray(np.tile(np.eye(chunk), (dim // chunk, 1)), BF)
    outs = [
        jax.ShapeDtypeStruct(o, F32)
        for o in ((2, chunk, 3 * width), (2, chunk, width), (2, chunk, hidden), (2, chunk, hidden), (chunk, PAIR))
    ]
    return pl.pallas_call(
        functools.partial(owner_kernel, shape),
        grid=(two.shape[0] // rows,),
        in_specs=[pl.BlockSpec((rows, m.shape[1]), lambda i: (i, 0)) for m in (two, one)]
        + [whole(m) for m in (pick, *sums)],
        out_specs=[whole(o) for o in outs],
        out_shape=outs,
        cost_estimate=BRIEF,
        name="owner_sums",
    )(two, one, pick, *sums)


def norm_stats(values):
    centred = values - jnp.mean(values, axis=-1, keepdims=True)
    inv = lax.rsqrt(jnp.mean(centred * centred, axis=-1, keepdims=True) + EPS_NORM)
    return centred * inv, inv


def norm_bwd(grad, unit, inv, gain):
    scaled = grad * gain
    along = jnp.mean(scaled * unit, axis=-1, keepdims=True)
    return inv * (scaled - jnp.mean(scaled, axis=-1, keepdims=True) - unit * along)


def column_sum(values):
    return jnp.sum(values, axis=0)


def advance(anchor, *moving):
    anchor = settle(anchor, *moving)
    going = [m for m in moving if m.left()]
    return launch(anchor, *going)


def local(
    layer_input,
    cotangent,
    lengths,
    w_qkv,
    w_out,
    w_up,
    w_down,
    vec_bias,
    norm_gain,
    bias_up,
    seg_pos,
):
    count = lax.axis_size("dp")
    bits = count.bit_length() - 1
    me = lax.axis_index("dp")
    part = lax.axis_index("tensor")
    seqs_here, half, dim = layer_input.shape
    full_len = 2 * half
    segments = full_len // SEG
    seg_half = half // SEG
    chunk = dim // count
    width = w_qkv.shape[3]
    hidden = w_up.shape[2]
    tile = hidden // PIECES
    three = 3 * PAIR
    orders = bit_orders(bits)
    swap_half = swap_tensor

    row_id = lax.broadcasted_iota(jnp.int32, (dim, dim), 0)
    col_id = lax.broadcasted_iota(jnp.int32, (dim, dim), 1)
    perm_hot = row_id == ((col_id // chunk) ^ me) * chunk + col_id % chunk
    perm = perm_hot.astype(BF)
    perm_f = perm_hot.astype(F32)

    def cut(matrix, size, p):
        return matrix[:, p * size : (p + 1) * size]

    def attn_piece(w_three, w_last, p):
        return jnp.concatenate([cut(w_three[:, k], PAIR, p) for k in range(3)] + [cut(w_last.T, PAIR, p)], axis=1)

    span = range(PIECES)
    one_q = Gather([attn_piece(w_qkv[0], w_out[0], p) for p in span], orders, bits, count)

    slot = me * 2 + part
    piece = vec_bias.shape[2]
    place = (
        lax.broadcasted_iota(jnp.int32, (piece, dim), 1)
        == lax.broadcasted_iota(jnp.int32, (piece, dim), 0) + slot * piece
    ).astype(F32)
    piece_up = bias_up.shape[1]
    hidden_all = piece_up * count * 2
    place_up = (
        lax.broadcasted_iota(jnp.int32, (piece_up, hidden_all), 1)
        == lax.broadcasted_iota(jnp.int32, (piece_up, hidden_all), 0) + slot * piece_up
    ).astype(F32)
    small_rows = jnp.concatenate(
        [vec_bias.reshape(-1, piece), norm_gain.reshape(-1, piece), seg_pos], axis=0
    )
    fold = hidden_all // dim
    small = jnp.concatenate(
        [dot_exact(small_rows, place), dot_exact(bias_up, place_up).reshape(2 * fold, dim)], axis=0
    )
    one_q.send()
    small = small + swap_tensor(small)
    for bit in range(bits - 3):
        small = small + swap_dp(small, bit, count)
    small = settle(small, one_q)
    small, w_qkv, w_out, w_up, w_down = tie(small, w_qkv, w_out, w_up, w_down)
    two_attn = jnp.concatenate([attn_piece(w_qkv[1], w_out[1], p) for p in span], axis=1)
    one_m = Gather([w_up[0], w_down[0].T, two_attn], orders[1:] + orders[:1], bits, count)
    two = Gather([w_up[1], w_down[1].T], orders[1:], bits, count)
    got = swap_dp(small, bits - 3, count)
    one_q.send()
    one_q.state[0], *one_m.state = tie(one_q.state[0], *one_m.state)
    one_m.send()
    got = settle(got, one_q)
    small = small + got
    got = swap_dp(small, bits - 2, count)
    one_q.send()
    got = settle(got, one_q, one_m)
    small = small + got
    last = swap_dp(small, bits - 1, count)
    small = launch(small, one_q)
    small = launch(small, one_m)
    while one_q.left() > 1:
        small = advance(small, one_q)
    x_own = dot_nn(layer_input[0], perm).astype(BF)
    x_full = jnp.concatenate([x_own, swap_half(x_own)], axis=0)
    x_full = settle(x_full, one_q, one_m)
    x_full, *two.state = tie(x_full, *two.state)
    x_full = launch(x_full, one_m)
    x_full = launch(x_full, two)
    x_full, last = tie(x_full, last)
    small = small + last

    plain = small[: small_rows.shape[0]]
    rel = dot_exact(plain, perm_f)

    bias_qkv, bias_hidden = own_biases(part, small, width, hidden)

    def block_vectors(block, order):
        base = 6 * block
        gain_at = 12 + 2 * block
        return dict(
            qkv=bias_qkv[block : block + 1],
            attn=order[base + 2],
            mlp=order[base + 3],
            shift_one=order[base + 4],
            shift_two=order[base + 5],
            gain_one=order[gain_at],
            gain_two=order[gain_at + 1],
            hidden=bias_hidden[block : block + 1],
        )

    v1, v2 = block_vectors(0, rel), block_vectors(1, rel)
    seg_rows = rel[16 : 16 + segments]

    length = lengths[0]
    seg_ids = jnp.concatenate(
        [part * seg_half + jnp.arange(seg_half), (1 - part) * seg_half + jnp.arange(seg_half)]
    ).astype(jnp.int32)
    seg_counts = jnp.clip(length - seg_ids * SEG, 0, SEG).astype(jnp.int32)
    cls_count = ((lengths + (SEG - 1)) // SEG).astype(jnp.int32)

    pad_rows = -segments % 16

    def padded(rows):
        return jnp.concatenate([rows, jnp.zeros((pad_rows, rows.shape[1]), rows.dtype)], axis=0)

    def turned(rows):
        return jnp.where(part == 0, rows, jnp.concatenate([rows[seg_half:], rows[:seg_half]], axis=0))

    def both_halves(own_rows):
        return turned(jnp.concatenate([own_rows, swap_half(own_rows)], axis=0))

    def own_half(rows):
        return jnp.where(part == 0, rows[:seg_half], rows[seg_half:segments])

    def firsts(rows):
        return rows.reshape(-1, SEG, rows.shape[-1])[:, 0]

    attn_r = one_q.results()
    w_qkv_r = jnp.concatenate([w[:, :three] for w in attn_r], axis=1)
    w_out_r = jnp.concatenate([w[:, three:] for w in attn_r], axis=1)
    qkv = (dot_nn(x_full, w_qkv_r) + v1["qkv"]).astype(BF)
    attended = attn_fwd(seg_counts, qkv)
    while one_m.left() > 1:
        attended = advance(attended, one_m)
    attended = advance(attended, two)
    partial_attn = dot_nt(attended, w_out_r).astype(BF)
    first_sum = (
        partial_attn[:half].astype(F32)
        + swap_half(partial_attn[half:]).astype(F32)
        + v1["attn"]
        + x_own.astype(F32)
    )
    unit_one, inv_one = norm_stats(first_sum)
    first = unit_one * v1["gain_one"] + v1["shift_one"]
    first_low = first.astype(BF)
    first_full = jnp.concatenate([first_low, swap_half(first_low)], axis=0)
    first_full = settle(first_full, one_m)
    w_up_r, w_down_r, two_attn_r = one_m.results()
    act, slope = up_gelu(first_full, w_up_r, v1["hidden"])
    while two.left() > 3:
        act = advance(act, two)
    act = advance(act, two)
    partial_mlp = dot_nt(act, w_down_r).astype(BF)
    second_sum = (
        partial_mlp[:half].astype(F32) + swap_half(partial_mlp[half:]).astype(F32) + v1["mlp"] + first
    )
    while two.left() > 1:
        second_sum = advance(second_sum, two)
    unit_two, inv_two = norm_stats(second_sum)
    first_out = unit_two * v1["gain_two"] + v1["shift_two"]

    row_in = lax.broadcasted_iota(jnp.int32, (half, 1), 0)
    valid = part * half + row_in < length
    is_cls = lax.broadcasted_iota(jnp.int32, (1, SEG, 1), 1) == 0

    def with_cls(rows, cls):
        return jnp.where(is_cls, cls[:, None, :], rows.reshape(seg_half, SEG, dim)).reshape(half, dim)

    cot = jnp.where(valid, cotangent[0], jnp.zeros_like(cotangent[0]))
    grad_y_low = dot_nn(cot, perm).astype(BF)
    grad_out = with_cls(grad_y_low.astype(F32), jnp.zeros((seg_half, dim), F32))
    g_second = norm_bwd(grad_out, unit_two, inv_two, v1["gain_two"])
    g_second_low = g_second.astype(BF)
    g_mlp = jnp.concatenate([g_second_low, swap_half(g_second_low)], axis=0)
    gpre = (dot_nn(g_mlp, w_down_r) * slope.astype(F32)).astype(BF)
    part_h = dot_nt(gpre, w_up_r).astype(BF)
    gw_up = dot_tn(first_full, gpre).astype(BF)
    gw_down = dot_tn(g_mlp, act).astype(BF)
    g_first = part_h[:half].astype(F32) + swap_half(part_h[half:]).astype(F32) + g_second
    g_first_sum = norm_bwd(g_first, unit_one, inv_one, v1["gain_one"])
    g_first_low = g_first_sum.astype(BF)
    g_attn = jnp.concatenate([g_first_low, swap_half(g_first_low)], axis=0)
    g_attended = dot_nn(g_attn, w_out_r).astype(BF)
    gw_out = dot_tn(g_attn, attended).astype(BF)
    early = Scatter([[gw_up], [gw_down]], orders[1:], bits, count)
    g_attended = launch(g_attended, early)

    sums_own = jnp.concatenate([firsts(second_sum), firsts(first_sum)], axis=0)
    sums_other = swap_half(sums_own)
    second_sum_1 = padded(turned(jnp.concatenate([sums_own[:seg_half], sums_other[:seg_half]], axis=0)))
    first_sum_1 = padded(turned(jnp.concatenate([sums_own[seg_half:], sums_other[seg_half:]], axis=0)))
    unit_two_1, inv_two_1 = norm_stats(second_sum_1)
    unit_one_1, inv_one_1 = norm_stats(first_sum_1)
    first_low_1 = (unit_one_1 * v1["gain_one"] + v1["shift_one"]).astype(BF)
    act_1, slope_1, att_1 = (turned(firsts(v)) for v in (act, slope, attended))
    cls_rel = unit_two_1 * v1["gain_two"] + v1["shift_two"]
    cls_in = padded(cls_rel[:segments] + seg_rows)
    g_c = padded(both_halves(firsts(grad_y_low))).astype(F32)

    cls_in, g_attended, gw_out = tie(cls_in, g_attended, gw_out)
    cls_in = settle(cls_in, two)
    attn_w = [(two_attn_r, p) for p in span]
    up_w, down_w = ([(w, p) for p in span] for w in two.results())
    cls_low = cls_in.astype(BF)
    rows_c = cls_in.shape[0]
    qkv_c, att_c, part_c = cls_call(
        cls_attn_kernel, "cls_attn", cls_count, cls_low, attn_w, tile, v2["qkv"],
        [((rows_c, 3 * width), BF), ((segments, width), BF), ((rows_c, dim), F32)],
    )
    sum_c1 = part_c + swap_half(part_c) + v2["attn"] + cls_in
    unit_c1, inv_c1 = norm_stats(sum_c1)
    first_c = unit_c1 * v2["gain_one"] + v2["shift_one"]
    first_c_low = first_c.astype(BF)
    act_c, slope_c, part_c2 = cls_call(
        cls_up_kernel, "cls_up", None, first_c_low, up_w + down_w, tile, v2["hidden"],
        [((segments, hidden), BF), ((rows_c, hidden), F32), ((rows_c, dim), F32)],
    )
    sum_c2 = part_c2 + swap_half(part_c2) + v2["mlp"] + first_c
    unit_c2, inv_c2 = norm_stats(sum_c2)
    cls_out = unit_c2 * v2["gain_two"] + v2["shift_two"]
    combined = jnp.where(valid, with_cls(first_out, own_half(cls_out)), 0.0).astype(BF)
    output = dot_nn(combined, perm).astype(BF)[None]

    g_second_c = norm_bwd(g_c, unit_c2, inv_c2, v2["gain_two"])
    g_mlp_c = g_second_c.astype(BF)
    back_outs = [((segments, hidden), BF), ((rows_c, dim), F32)]
    gpre_c, part_g1 = cls_call(
        cls_up_back_kernel, "cls_up_back", None, g_mlp_c, up_w + down_w, tile, slope_c, back_outs
    )
    g_first_c = part_g1 + swap_half(part_g1) + g_second_c
    g_sum_c = norm_bwd(g_first_c, unit_c1, inv_c1, v2["gain_one"])
    g_attn_c = g_sum_c.astype(BF)
    gqkv_c, part_g2 = cls_call(
        cls_attn_back_kernel, "cls_attn_back", cls_count, g_attn_c, attn_w, tile, qkv_c,
        [((segments, 3 * width), BF), ((rows_c, dim), F32)],
    )
    g_cls_in = part_g2 + swap_half(part_g2) + g_sum_c
    near_two = tuple(f[:segments] for f in (cls_low, first_c_low, g_attn_c, g_mlp_c))
    far_two = (act_c, gpre_c, att_c, gqkv_c) + near_two
    wide_two = Gather([jnp.concatenate(far_two, axis=1)], orders[:1], bits, count)
    while early.left() > 3:
        g_cls_in = advance(g_cls_in, early)
    g_cls_in = launch(g_cls_in, wide_two)

    g_second_1 = norm_bwd(g_cls_in, unit_two_1, inv_two_1, v1["gain_two"])
    g_mlp_1 = g_second_1.astype(BF)
    gpre_1, part_1 = cls_call(
        cls_up_back_kernel, "cls_up_back", None, g_mlp_1, [(w, p) for w in (w_up_r, w_down_r) for p in span], tile,
        padded(slope_1.astype(F32)), back_outs
    )
    part_1 = advance(part_1, wide_two)
    g_first_1 = part_1 + swap_half(part_1) + g_second_1
    g_sum_1 = norm_bwd(g_first_1, unit_one_1, inv_one_1, v1["gain_one"])
    g_attn_1 = g_sum_1.astype(BF)
    g_att_1 = turned(dot_nn(g_attn_1, w_out_r).astype(BF)[:segments])

    near_one = tuple(f[:segments] for f in (first_low_1, g_mlp_1, g_attn_1))
    far_one = (act_1, gpre_1, att_1) + near_one
    wide_one = Gather([jnp.concatenate(far_one, axis=1)], orders[1:2], bits, count)
    g_att_1 = advance(g_att_1, early, wide_two)
    g_att_1 = launch(g_att_1, wide_one)

    scale_one = 1.0 / math.sqrt(seqs_here * count * full_len)
    scale_two = 1.0 / math.sqrt(seqs_here * count * segments)

    def spread(values, total):
        zero = jnp.zeros((total - values.shape[0],), F32)
        return jnp.where(part == 0, jnp.concatenate([values, zero]), jnp.concatenate([zero, values]))

    def both_sums(rows, cls):
        return (column_sum(rows) + column_sum(own_half(cls))) * scale_one

    def cls_sums(cls):
        return column_sum(own_half(cls)) * scale_two

    sums_c = column_sum(gqkv_c.astype(F32)).reshape(PIECES, 3, PAIR) * scale_two
    rel_rows = jnp.stack(
        [
            both_sums(g_first_sum, g_sum_1),
            both_sums(g_second, g_second_1),
            both_sums(g_first, g_first_1),
            both_sums(grad_out, g_cls_in),
            cls_sums(g_sum_c),
            cls_sums(g_second_c),
            cls_sums(g_first_c),
            cls_sums(g_c),
            both_sums(g_first * unit_one, g_first_1 * unit_one_1),
            both_sums(grad_out * unit_two, g_cls_in * unit_two_1),
            cls_sums(g_first_c * unit_c1),
            cls_sums(g_c * unit_c2),
        ]
    )
    zeros_half = jnp.zeros((seg_half, dim), F32)
    cls_part = own_half(g_cls_in) * scale_two
    seg_grad = jnp.where(
        part == 0,
        jnp.concatenate([cls_part, zeros_half], axis=0),
        jnp.concatenate([zeros_half, cls_part], axis=0),
    )
    up_rows = jnp.stack(
        [
            spread((dot_nn(jnp.ones((16, 2 * half), BF), gpre)[0] + column_sum(gpre_1.astype(F32))) * scale_one, hidden_all),
            spread(column_sum(gpre_c.astype(F32)) * scale_two, hidden_all),
        ]
    )
    per_row = 2 * hidden_all // dim
    by_owner = up_rows.reshape(2, count, -1).transpose(1, 0, 2).reshape(dim, per_row)
    plain_rows = jnp.stack([spread(sums_c[:, k].reshape(-1), dim) for k in (0, 2)])
    canon = dot_exact(jnp.concatenate([plain_rows, by_owner.T], axis=0), perm_f)
    small_rows = jnp.concatenate([rel_rows, seg_grad, canon], axis=0)
    small_rows = small_rows + swap_tensor(small_rows)
    filler = jnp.zeros((PAIR - small_rows.shape[0] - 2, dim), F32)
    small_cols = jnp.concatenate([small_rows, filler], axis=0).T.astype(BF)
    g_att_1, small_cols, output = tie(g_att_1, small_cols, output)

    gqkv, gqkv_sums = attn_bwd(seg_counts, qkv, g_attended, g_att_1)
    gw_qkv = dot_tn(x_full, gqkv).astype(BF)
    sums_o = gqkv_sums.reshape(PIECES, 3, PAIR) * scale_one
    bias_own = jnp.stack([spread(sums_o[:, k].reshape(-1), dim) for k in (0, 2)])
    bias_cols = dot_exact(bias_own + swap_tensor(bias_own), perm_f).T.astype(BF)
    small_cols = jnp.concatenate([small_cols, bias_cols], axis=1)
    late = Scatter(
        [[cut(gw_qkv, three, p), cut(gw_out, PAIR, p)] + [small_cols] * (p == 0) for p in span], orders, bits, count
    )
    gqkv = launch(gqkv, late)
    wides = (wide_two, wide_one)
    gqkv = advance(gqkv, early, wide_one)
    part_x = dot_nt(gqkv, w_qkv_r).astype(BF)

    part_x = advance(part_x, late, wide_two)
    part_x = advance(part_x, wide_one)
    g_first_all = with_cls(g_first_sum, own_half(g_sum_1))
    g_in = part_x[:half].astype(F32) + swap_half(part_x[half:]).astype(F32) + g_first_all
    g_in_high = lax.reduce_precision(g_in, 8, 7)
    grad_input = (dot_nn(g_in_high.astype(BF), perm) + dot_nn((g_in - g_in_high).astype(BF), perm))[None]
    anchor = jnp.zeros((), F32)
    movers = (late, early, *wides)
    while any(m.left() > 1 for m in movers):
        for m in movers:
            if m.left() > 1:
                anchor = advance(anchor, m)
    anchor = settle(anchor, late, early, *wides)

    shape = (width, hidden, dim, chunk, segments, scale_one, scale_two)
    grad_three, grad_last, grad_w_up, grad_down, small_own = owner_sums(
        shape, wide_two.results()[0], wide_one.results()[0], early.pairs() + late.pairs()
    )
    grad_w_qkv = grad_three.reshape(2, chunk, 3, width)
    grad_w_out = grad_last.transpose(0, 2, 1)
    grad_w_down = grad_down.transpose(0, 2, 1)

    mine = small_own.T
    rows_own = jnp.where(part == 0, mine[:, :piece], mine[:, piece:])
    vecs = rows_own[:12]
    grad_vec = jnp.concatenate([rows_own[PAIR - 2 :], vecs[:4], rows_own[20:22], vecs[4:8]], axis=0).reshape(2, 6, piece)
    grad_gain = vecs[8:].reshape(2, 2, piece)
    grad_seg = rows_own[12:20]
    up_own = mine[22 : 22 + per_row].T.reshape(2, 2, piece_up)
    grad_up_vec = jnp.where(part == 0, up_own[:, 0], up_own[:, 1])
    return (
        output,
        grad_input,
        grad_w_qkv,
        grad_w_out,
        grad_w_up,
        grad_w_down,
        grad_vec,
        grad_gain,
        grad_up_vec,
        grad_seg,
    )


def solution(mesh):
    return jax.shard_map(
        local,
        mesh=mesh,
        in_specs=(
            P("dp", "tensor", None),
            P("dp", "tensor", None),
            P("dp"),
            P(None, "dp", None, "tensor"),
            P(None, "tensor", "dp"),
            P(None, "dp", "tensor"),
            P(None, "tensor", "dp"),
            P(None, None, ("dp", "tensor")),
            P(None, None, ("dp", "tensor")),
            P(None, ("dp", "tensor")),
            P(None, ("dp", "tensor")),
        ),
        out_specs=(
            P("dp", "tensor", None),
            P("dp", "tensor", None),
            P(None, "dp", None, "tensor"),
            P(None, "tensor", "dp"),
            P(None, "dp", "tensor"),
            P(None, "tensor", "dp"),
            P(None, None, ("dp", "tensor")),
            P(None, None, ("dp", "tensor")),
            P(None, ("dp", "tensor")),
            P(None, ("dp", "tensor")),
        ),
        check_vma=False,
    )
```

```python
import functools
import math

import jax
import jax.numpy as jnp
import numpy as np
from jax import lax
from jax.experimental import pallas as pl
from jax.experimental.pallas import tpu as pltpu
from jax.sharding import PartitionSpec as P

HD = 64
SEG = 128
NEG_FILL = -1000000000.0
EPS_NORM = 1e-06
BF = jnp.bfloat16
F32 = jnp.float32
INV_SQRT2 = 1.0 / math.sqrt(2.0)
INV_SQRT2PI = 1.0 / math.sqrt(2.0 * math.pi)
SM_SCALE = HD ** (-0.5)
PAIR = 2 * HD
PIECES = 3
BRIEF = pl.CostEstimate(flops=1, bytes_accessed=1, transcendentals=0)


def dot_nn(a, b):
    return lax.dot_general(a, b, (((1,), (0,)), ((), ())), preferred_element_type=F32)


def dot_nt(a, b):
    return lax.dot_general(a, b, (((1,), (1,)), ((), ())), preferred_element_type=F32)


def dot_tn(a, b):
    return lax.dot_general(a, b, (((0,), (0,)), ((), ())), preferred_element_type=F32)


def dot_exact(a, b):
    return lax.dot_general(
        a, b, (((1,), (0,)), ((), ())), precision=lax.Precision.HIGHEST, preferred_element_type=F32
    )


def swap_dp(values, bit, count):
    return lax.ppermute(values, "dp", [(i, i ^ (1 << bit)) for i in range(count)])


def swap_tensor(values):
    return lax.ppermute(values, "tensor", [(0, 1), (1, 0)])


def bit_orders(bits):
    if bits == 4:
        return ((3, 2, 0, 1), (3, 1, 2, 0), (3, 0, 1, 2))
    base = tuple(range(bits))
    return (base, base[1:] + base[:1], base[2:] + base[:2])


def tie(*values):
    return lax.optimization_barrier(values)


def join(low, high, bit, bits):
    return jnp.concatenate([low, high], axis=bits - 1 - bit)


class Gather:
    def __init__(self, pieces, orders, bits, count):
        self.state = [u.reshape((1,) * bits + u.shape) for u in pieces]
        self.orders, self.bits, self.count, self.step = orders, bits, count, 0

    def send(self):
        self.flying = [
            swap_dp(v, self.orders[i][self.step], self.count) for i, v in enumerate(self.state)
        ]

    def land(self):
        self.state = [
            join(v, f, self.orders[i][self.step], self.bits)
            for i, (v, f) in enumerate(zip(self.state, self.flying))
        ]
        self.step += 1

    def left(self):
        return self.bits - self.step

    def results(self):
        return [v.reshape((-1, v.shape[-1])) for v in self.state]


def half_of(values, axis, index):
    return lax.index_in_dim(values, index, axis, keepdims=True)


class Scatter:
    def __init__(self, pieces, orders, bits, count):
        self.bits, self.count, self.step = bits, count, 0
        self.orders = [tuple(reversed(o)) for o in orders]
        self.parts = [[[m.reshape((2,) * bits + (-1, m.shape[-1])) for m in piece]] for piece in pieces]

    def half(self, which, index):
        axis = self.bits - 1 - self.orders[which][self.step]
        cut = [
            jnp.concatenate([half_of(m, axis, index) for m in part], axis=-1).astype(F32)
            for part in self.parts[which]
        ]
        return sum(cut[1:], cut[0]).astype(BF)

    def prepare(self):
        self.leaving = [self.half(i, 1) for i in range(len(self.parts))]

    def send(self):
        self.flying = [
            swap_dp(v, self.orders[i][self.step], self.count) for i, v in enumerate(self.leaving)
        ]
        self.kept = [self.half(i, 0) for i in range(len(self.parts))]

    def land(self):
        self.parts = [[[k], [f]] for k, f in zip(self.kept, self.flying)]
        self.step += 1

    def left(self):
        return self.bits - self.step

    def pairs(self):
        return [side[0].reshape((-1, side[0].shape[-1])) for part in self.parts for side in part]


def settle(anchor, *moving):
    flat = [f for m in moving for f in m.flying]
    anchor, *flat = tie(anchor, *flat)
    for m in moving:
        m.flying = flat[: len(m.flying)]
        flat = flat[len(m.flying) :]
        m.land()
    return anchor


def launch(anchor, *moving):
    for m in moving:
        if isinstance(m, Scatter):
            m.prepare()
            anchor, *m.leaving = tie(anchor, *m.leaving)
        elif isinstance(m, Gather):
            anchor, *m.state = tie(anchor, *m.state)
        else:
            anchor, m.state = tie(anchor, m.state)
        m.send()
    return anchor


def pair_masks(rows):
    lane = lax.broadcasted_iota(jnp.int32, (rows, PAIR), 1)
    return lane < HD


def stack_heads(two, low_half):
    zero = jnp.zeros_like(two)
    return jnp.concatenate([jnp.where(low_half, two, zero), jnp.where(low_half, zero, two)], axis=0)


def merge_heads(stacked, low_half, rows):
    return jnp.where(low_half, stacked[:rows], stacked[rows:])


def pair_probs(q_stack, key_two, allowed):
    scores = dot_nt(q_stack, key_two) * SM_SCALE
    scores = jnp.where(allowed, scores, NEG_FILL)
    expo = jnp.exp(scores - jnp.max(scores, axis=-1, keepdims=True))
    return expo * (1.0 / jnp.sum(expo, axis=-1, keepdims=True))


def row_window(rows):
    return [pl.BlockSpec((SEG, cols), lambda i, c: (i, 0)) for cols in rows]


def attn_fwd_kernel(count_ref, qkv_ref, out_ref):
    rows = qkv_ref.shape[0]
    low_half = pair_masks(rows)
    allowed = lax.broadcasted_iota(jnp.int32, (2 * rows, rows), 1) < count_ref[pl.program_id(0)]
    for pair in range(out_ref.shape[1] // PAIR):
        at = 3 * pair * PAIR
        q_stack = stack_heads(qkv_ref[:, at : at + PAIR], low_half)
        probs = pair_probs(q_stack, qkv_ref[:, at + PAIR : at + 2 * PAIR], allowed)
        mixed = dot_nn(probs.astype(BF), qkv_ref[:, at + 2 * PAIR : at + 3 * PAIR])
        out_ref[:, pair * PAIR : (pair + 1) * PAIR] = merge_heads(mixed, low_half, rows).astype(BF)


def pair_bwd(qkv, grad, allowed, low_half):
    rows = grad.shape[0]
    key_two = qkv[:, PAIR : 2 * PAIR]
    q_stack = stack_heads(qkv[:, :PAIR], low_half)
    g_stack = stack_heads(grad, low_half)
    probs = pair_probs(q_stack, key_two, allowed)
    grad_probs = dot_nt(g_stack, qkv[:, 2 * PAIR :])
    inner = jnp.sum(grad_probs * probs, axis=-1, keepdims=True)
    grad_scores = jnp.where(allowed, probs * (grad_probs - inner), 0.0).astype(BF)
    return (
        merge_heads(dot_nn(grad_scores, key_two), low_half, rows) * SM_SCALE,
        dot_tn(grad_scores, q_stack) * SM_SCALE,
        dot_tn(probs.astype(BF), g_stack),
    )


def attn_bwd_kernel(count_ref, qkv_ref, grad_ref, first_ref, out_ref, sums_ref):
    rows = qkv_ref.shape[0]
    low_half = pair_masks(rows)
    allowed = lax.broadcasted_iota(jnp.int32, (2 * rows, rows), 1) < count_ref[pl.program_id(0)]
    is_first = lax.broadcasted_iota(jnp.int32, (rows, PAIR), 0) == 0

    @pl.when(pl.program_id(0) == 0)
    def _():
        sums_ref[...] = jnp.zeros_like(sums_ref)

    for pair in range(grad_ref.shape[1] // PAIR):
        at = 3 * pair * PAIR
        span = slice(pair * PAIR, (pair + 1) * PAIR)
        grad = jnp.where(is_first, first_ref[0, :, span], grad_ref[:, span].astype(F32)).astype(BF)
        for k, values in enumerate(pair_bwd(qkv_ref[:, at : at + 3 * PAIR], grad, allowed, low_half)):
            low = values.astype(BF)
            to = slice(at + k * PAIR, at + (k + 1) * PAIR)
            out_ref[:, to] = low
            sums_ref[:, to] += jnp.sum(low.astype(F32), axis=0, keepdims=True)


def attn_fwd(counts, qkv):
    rows, three = qkv.shape
    width = three // 3
    return pl.pallas_call(
        attn_fwd_kernel,
        grid_spec=pltpu.PrefetchScalarGridSpec(
            num_scalar_prefetch=1,
            grid=(rows // SEG,),
            in_specs=row_window([three]),
            out_specs=row_window([width])[0],
        ),
        out_shape=jax.ShapeDtypeStruct((rows, width), BF),
        cost_estimate=BRIEF,
        name="attn_fwd",
    )(counts, qkv)


def attn_bwd(counts, qkv, grad, grad_first):
    rows, three = qkv.shape
    width = three // 3
    return pl.pallas_call(
        attn_bwd_kernel,
        grid_spec=pltpu.PrefetchScalarGridSpec(
            num_scalar_prefetch=1,
            grid=(rows // SEG,),
            in_specs=row_window([three, width]) + [pl.BlockSpec((1, 1, width), lambda i, c: (i, 0, 0))],
            out_specs=row_window([three]) + [pl.BlockSpec((1, three), lambda i, c: (0, 0))],
        ),
        out_shape=[jax.ShapeDtypeStruct((rows, three), BF), jax.ShapeDtypeStruct((1, three), F32)],
        cost_estimate=BRIEF,
        name="attn_bwd",
    )(counts, qkv, grad, grad_first.astype(F32)[:, None, :])


def gelu_pair(pre):
    cdf = 0.5 * (1.0 + lax.erf(pre * INV_SQRT2))
    return pre * cdf, cdf + pre * (jnp.exp(-0.5 * pre * pre) * INV_SQRT2PI)


def up_kernel(rows_ref, w_ref, bias_ref, act_ref, slope_ref):
    act, slope = gelu_pair(dot_nn(rows_ref[...], w_ref[...]) + bias_ref[...])
    act_ref[...] = act.astype(BF)
    slope_ref[...] = slope.astype(BF)


def up_gelu(rows, w_up, bias):
    total, dim = rows.shape
    hidden = w_up.shape[1]
    tile_r = min(256, total)
    tile_h = min(512, hidden)
    spec_out = pl.BlockSpec((tile_r, tile_h), lambda j, i: (i, j))
    return pl.pallas_call(
        up_kernel,
        grid=(hidden // tile_h, total // tile_r),
        in_specs=[
            pl.BlockSpec((tile_r, dim), lambda j, i: (i, 0)),
            pl.BlockSpec((dim, tile_h), lambda j, i: (0, j)),
            pl.BlockSpec((1, tile_h), lambda j, i: (0, j)),
        ],
        out_specs=[spec_out, spec_out],
        out_shape=[jax.ShapeDtypeStruct((total, hidden), BF)] * 2,
        cost_estimate=BRIEF,
        name="up_gelu",
    )(rows, w_up, bias)


def cls_attn_kernel(count_ref, rows_ref, w0, w1, w2, bias_ref, qkv_ref, att_ref, sum_ref):
    rows = rows_ref.shape[0]
    low_half = pair_masks(rows)
    allowed = lax.broadcasted_iota(jnp.int32, (2 * rows, rows), 1) < count_ref[0]
    total = jnp.zeros(sum_ref.shape, F32)
    for p, w in enumerate((w0, w1, w2)):
        span = slice(3 * p * PAIR, 3 * (p + 1) * PAIR)
        qkv = (dot_nn(rows_ref[...], w[:, : 3 * PAIR]) + bias_ref[:, span]).astype(BF)
        qkv_ref[:, span] = qkv
        probs = pair_probs(stack_heads(qkv[:, :PAIR], low_half), qkv[:, PAIR : 2 * PAIR], allowed)
        att = merge_heads(dot_nn(probs.astype(BF), qkv[:, 2 * PAIR :]), low_half, rows).astype(BF)
        att_ref[:, p * PAIR : (p + 1) * PAIR] = att[: att_ref.shape[0]]
        total += dot_nt(att, w[:, 3 * PAIR :])
    sum_ref[...] = total


def cls_attn_back_kernel(count_ref, grad_ref, w0, w1, w2, qkv_ref, out_ref, sum_ref):
    rows = grad_ref.shape[0]
    low_half = pair_masks(rows)
    allowed = lax.broadcasted_iota(jnp.int32, (2 * rows, rows), 1) < count_ref[0]
    total = jnp.zeros(sum_ref.shape, F32)
    for p, w in enumerate((w0, w1, w2)):
        span = slice(3 * p * PAIR, 3 * (p + 1) * PAIR)
        grad = dot_nn(grad_ref[...], w[:, 3 * PAIR :]).astype(BF)
        low = jnp.concatenate(pair_bwd(qkv_ref[:, span], grad, allowed, low_half), axis=1).astype(BF)
        out_ref[:, span] = low[: out_ref.shape[0]]
        total += dot_nt(low, w[:, : 3 * PAIR])
    sum_ref[...] = total


def cls_up_kernel(rows_ref, u0, u1, u2, d0, d1, d2, bias_ref, act_ref, slope_ref, sum_ref):
    tile = u0.shape[1]
    total = jnp.zeros(sum_ref.shape, F32)
    for p, (u, d) in enumerate(((u0, d0), (u1, d1), (u2, d2))):
        span = slice(p * tile, (p + 1) * tile)
        act, slope = gelu_pair(dot_nn(rows_ref[...], u[...]) + bias_ref[:, span])
        low = act.astype(BF)
        act_ref[:, span] = low[: act_ref.shape[0]]
        slope_ref[:, span] = slope
        total += dot_nt(low, d[...])
    sum_ref[...] = total


def cls_up_back_kernel(rows_ref, u0, u1, u2, d0, d1, d2, slope_ref, out_ref, sum_ref):
    tile = u0.shape[1]
    total = jnp.zeros(sum_ref.shape, F32)
    for p, (u, d) in enumerate(((u0, d0), (u1, d1), (u2, d2))):
        span = slice(p * tile, (p + 1) * tile)
        low = (dot_nn(rows_ref[...], d[...]) * slope_ref[:, span]).astype(BF)
        out_ref[:, span] = low[: out_ref.shape[0]]
        total += dot_nt(low, u[...])
    sum_ref[...] = total


def block_at(at, *_):
    return 0, at


def whole(array):
    return pl.BlockSpec(array.shape, lambda *_: (0,) * array.ndim)


def cls_call(kernel, name, count, before, weights, tile, after, outs):
    shapes = [jax.ShapeDtypeStruct(*o) for o in outs]
    dim = weights[0][0].shape[0]
    scalars = [] if count is None else [count]
    return pl.pallas_call(
        kernel,
        grid_spec=pltpu.PrefetchScalarGridSpec(
            num_scalar_prefetch=len(scalars),
            grid=(1,),
            in_specs=[whole(before)]
            + [pl.BlockSpec((dim, tile), functools.partial(block_at, at)) for _, at in weights]
            + [whole(after)],
            out_specs=[whole(o) for o in shapes],
        ),
        out_shape=shapes,
        cost_estimate=BRIEF,
        name=name,
    )(*scalars, before, *[w for w, _ in weights], after)


def own_bias_kernel(part_ref, rows_ref, qkv_ref, hidden_ref):
    width = rows_ref.shape[1] // 2
    first = part_ref[0] == 0
    fold = (rows_ref.shape[0] - 24) // 2

    def own(row, at, size):
        return jnp.where(first, rows_ref[row : row + 1, at : at + size], rows_ref[row : row + 1, width + at : width + at + size])

    for block in range(2):
        for p in range(PIECES):
            parts = (own(6 * block, p * PAIR, PAIR), jnp.zeros((1, PAIR), F32), own(6 * block + 1, p * PAIR, PAIR))
            for k, value in enumerate(parts):
                at = (3 * p + k) * PAIR
                qkv_ref[block : block + 1, at : at + PAIR] = value
        base = 24 + fold * block
        for k in range(fold // 2):
            low, high = base + k, base + fold // 2 + k
            value = jnp.where(first, rows_ref[low : low + 1, :], rows_ref[high : high + 1, :])
            hidden_ref[block : block + 1, 2 * width * k : 2 * width * (k + 1)] = value


def own_biases(part, rows, width, hidden):
    outs = [jax.ShapeDtypeStruct((2, 3 * width), F32), jax.ShapeDtypeStruct((2, hidden), F32)]
    return pl.pallas_call(
        own_bias_kernel,
        grid_spec=pltpu.PrefetchScalarGridSpec(
            num_scalar_prefetch=1,
            grid=(1,),
            in_specs=[whole(rows)],
            out_specs=[whole(o) for o in outs],
        ),
        out_shape=outs,
        cost_estimate=BRIEF,
        name="own_biases",
    )(part.reshape(1).astype(jnp.int32), rows)


def owner_kernel(
    shape, two_ref, one_ref, pick_ref, uk, uf, dk, df, l0k, l0f, l1k, l1f, l2k, l2f,
    qkv_ref, out_ref, up_ref, down_ref, small_ref,
):
    width, hidden, dim, chunk, segments, scale_one, scale_two = shape
    rows = two_ref.shape[0]
    three = 3 * PAIR

    def put_kinds(block, values, add):
        for p in range(PIECES):
            for k in range(3):
                to = slice(k * width + p * PAIR, k * width + (p + 1) * PAIR)
                got = values[p][:, k * PAIR : (k + 1) * PAIR]
                qkv_ref[block, :, to] = qkv_ref[block, :, to] + got if add else got

    @pl.when(pl.program_id(0) == 0)
    def _():
        both = lambda a, b: (a[...].astype(F32) + b[...].astype(F32)) * scale_one
        up_ref[0] = both(uk, uf)
        down_ref[0] = both(dk, df)
        up_ref[1] = jnp.zeros_like(up_ref[1])
        down_ref[1] = jnp.zeros_like(down_ref[1])
        out_ref[1] = jnp.zeros_like(out_ref[1])
        qkv_ref[1] = jnp.zeros_like(qkv_ref[1])
        late = [both(a, b) for a, b in ((l0k, l0f), (l1k, l1f), (l2k, l2f))]
        put_kinds(0, late, False)
        for p in range(PIECES):
            out_ref[0, :, p * PAIR : (p + 1) * PAIR] = late[p][:, three : three + PAIR]
        small_ref[...] = l0k[:, three + PAIR :].astype(F32) + l0f[:, three + PAIR :].astype(F32)

    block = (lax.broadcasted_iota(jnp.int32, (rows, dim), 0) + rows * pl.program_id(0)) // segments
    col = lax.broadcasted_iota(jnp.int32, (rows, dim), 1)
    mine = (col >= block * chunk) & (col < block * chunk + chunk)

    def near(ref, at):
        picked = jnp.where(mine, ref[:, at : at + dim].astype(F32), 0.0).astype(BF)
        return dot_nn(picked, pick_ref[...]).astype(BF)

    at_pre, at_att, at_qkv = hidden, 2 * hidden, 2 * hidden + width
    at_two, at_one = at_qkv + 3 * width, at_qkv
    in_f, first_f, g_attn_f, g_mlp_f = (near(two_ref, at_two + k * dim) for k in range(4))
    first_1, g_mlp_1, g_attn_1 = (near(one_ref, at_one + k * dim) for k in range(3))
    up_ref[0] += dot_tn(first_1, one_ref[:, at_pre:at_att]) * scale_one
    down_ref[0] += dot_tn(g_mlp_1, one_ref[:, :at_pre]) * scale_one
    out_ref[0] += dot_tn(g_attn_1, one_ref[:, at_att:at_qkv]) * scale_one
    up_ref[1] += dot_tn(first_f, two_ref[:, at_pre:at_att]) * scale_two
    down_ref[1] += dot_tn(g_mlp_f, two_ref[:, :at_pre]) * scale_two
    out_ref[1] += dot_tn(g_attn_f, two_ref[:, at_att:at_qkv]) * scale_two
    grad = dot_tn(in_f, two_ref[:, at_qkv:at_two]) * scale_two
    put_kinds(1, [grad[:, p * three : (p + 1) * three] for p in range(PIECES)], True)


def owner_sums(shape, two, one, sums):
    width, hidden, dim, chunk, segments, _, _ = shape
    rows = min(128, two.shape[0])
    pick = jnp.asarray(np.tile(np.eye(chunk), (dim // chunk, 1)), BF)
    outs = [
        jax.ShapeDtypeStruct(o, F32)
        for o in ((2, chunk, 3 * width), (2, chunk, width), (2, chunk, hidden), (2, chunk, hidden), (chunk, PAIR))
    ]
    return pl.pallas_call(
        functools.partial(owner_kernel, shape),
        grid=(two.shape[0] // rows,),
        in_specs=[pl.BlockSpec((rows, m.shape[1]), lambda i: (i, 0)) for m in (two, one)]
        + [whole(m) for m in (pick, *sums)],
        out_specs=[whole(o) for o in outs],
        out_shape=outs,
        cost_estimate=BRIEF,
        name="owner_sums",
    )(two, one, pick, *sums)


def norm_stats(values):
    centred = values - jnp.mean(values, axis=-1, keepdims=True)
    inv = lax.rsqrt(jnp.mean(centred * centred, axis=-1, keepdims=True) + EPS_NORM)
    return centred * inv, inv


def norm_bwd(grad, unit, inv, gain):
    scaled = grad * gain
    along = jnp.mean(scaled * unit, axis=-1, keepdims=True)
    return inv * (scaled - jnp.mean(scaled, axis=-1, keepdims=True) - unit * along)


def column_sum(values):
    return jnp.sum(values, axis=0)


def advance(anchor, *moving):
    anchor = settle(anchor, *moving)
    going = [m for m in moving if m.left()]
    return launch(anchor, *going)


def local(
    layer_input,
    cotangent,
    lengths,
    w_qkv,
    w_out,
    w_up,
    w_down,
    vec_bias,
    norm_gain,
    bias_up,
    seg_pos,
):
    count = lax.axis_size("dp")
    bits = count.bit_length() - 1
    me = lax.axis_index("dp")
    part = lax.axis_index("tensor")
    seqs_here, half, dim = layer_input.shape
    full_len = 2 * half
    segments = full_len // SEG
    seg_half = half // SEG
    chunk = dim // count
    width = w_qkv.shape[3]
    hidden = w_up.shape[2]
    tile = hidden // PIECES
    three = 3 * PAIR
    orders = bit_orders(bits)
    swap_half = swap_tensor

    row_id = lax.broadcasted_iota(jnp.int32, (dim, dim), 0)
    col_id = lax.broadcasted_iota(jnp.int32, (dim, dim), 1)
    perm_hot = row_id == ((col_id // chunk) ^ me) * chunk + col_id % chunk
    perm = perm_hot.astype(BF)
    perm_f = perm_hot.astype(F32)

    def cut(matrix, size, p):
        return matrix[:, p * size : (p + 1) * size]

    def attn_piece(w_three, w_last, p):
        return jnp.concatenate([cut(w_three[:, k], PAIR, p) for k in range(3)] + [cut(w_last.T, PAIR, p)], axis=1)

    span = range(PIECES)
    one_q = Gather([attn_piece(w_qkv[0], w_out[0], p) for p in span], orders, bits, count)

    slot = me * 2 + part
    piece = vec_bias.shape[2]
    place = (
        lax.broadcasted_iota(jnp.int32, (piece, dim), 1)
        == lax.broadcasted_iota(jnp.int32, (piece, dim), 0) + slot * piece
    ).astype(F32)
    piece_up = bias_up.shape[1]
    hidden_all = piece_up * count * 2
    place_up = (
        lax.broadcasted_iota(jnp.int32, (piece_up, hidden_all), 1)
        == lax.broadcasted_iota(jnp.int32, (piece_up, hidden_all), 0) + slot * piece_up
    ).astype(F32)
    small_rows = jnp.concatenate(
        [vec_bias.reshape(-1, piece), norm_gain.reshape(-1, piece), seg_pos], axis=0
    )
    fold = hidden_all // dim
    small = jnp.concatenate(
        [dot_exact(small_rows, place), dot_exact(bias_up, place_up).reshape(2 * fold, dim)], axis=0
    )
    one_q.send()
    small = small + swap_tensor(small)
    for bit in range(bits - 3):
        small = small + swap_dp(small, bit, count)
    small = settle(small, one_q)
    small, w_qkv, w_out, w_up, w_down = tie(small, w_qkv, w_out, w_up, w_down)
    two_attn = jnp.concatenate([attn_piece(w_qkv[1], w_out[1], p) for p in span], axis=1)
    one_m = Gather([w_up[0], w_down[0].T, two_attn], orders[1:] + orders[:1], bits, count)
    two = Gather([w_up[1], w_down[1].T], orders[1:], bits, count)
    got = swap_dp(small, bits - 3, count)
    one_q.send()
    got = settle(got, one_q)
    small = small + got
    got = swap_dp(small, bits - 2, count)
    one_q.send()
    one_q.state[0], *one_m.state = tie(one_q.state[0], *one_m.state)
    one_m.send()
    got = settle(got, one_q)
    small = small + got
    last = swap_dp(small, bits - 1, count)
    small = launch(small, one_q)
    while one_q.left() > 1:
        small = advance(small, one_q)
    x_own = dot_nn(layer_input[0], perm).astype(BF)
    x_full = jnp.concatenate([x_own, swap_half(x_own)], axis=0)
    x_full = settle(x_full, one_q, one_m)
    x_full = launch(x_full, one_m)
    x_full, last = tie(x_full, last)
    small = small + last

    plain = small[: small_rows.shape[0]]
    rel = dot_exact(plain, perm_f)

    bias_qkv, bias_hidden = own_biases(part, small, width, hidden)

    def block_vectors(block, order):
        base = 6 * block
        gain_at = 12 + 2 * block
        return dict(
            qkv=bias_qkv[block : block + 1],
            attn=order[base + 2],
            mlp=order[base + 3],
            shift_one=order[base + 4],
            shift_two=order[base + 5],
            gain_one=order[gain_at],
            gain_two=order[gain_at + 1],
            hidden=bias_hidden[block : block + 1],
        )

    v1, v2 = block_vectors(0, rel), block_vectors(1, rel)
    seg_rows = rel[16 : 16 + segments]

    length = lengths[0]
    seg_ids = jnp.concatenate(
        [part * seg_half + jnp.arange(seg_half), (1 - part) * seg_half + jnp.arange(seg_half)]
    ).astype(jnp.int32)
    seg_counts = jnp.clip(length - seg_ids * SEG, 0, SEG).astype(jnp.int32)
    cls_count = ((lengths + (SEG - 1)) // SEG).astype(jnp.int32)

    pad_rows = -segments % 16

    def padded(rows):
        return jnp.concatenate([rows, jnp.zeros((pad_rows, rows.shape[1]), rows.dtype)], axis=0)

    def turned(rows):
        return jnp.where(part == 0, rows, jnp.concatenate([rows[seg_half:], rows[:seg_half]], axis=0))

    def both_halves(own_rows):
        return turned(jnp.concatenate([own_rows, swap_half(own_rows)], axis=0))

    def own_half(rows):
        return jnp.where(part == 0, rows[:seg_half], rows[seg_half:segments])

    def firsts(rows):
        return rows.reshape(-1, SEG, rows.shape[-1])[:, 0]

    attn_r = one_q.results()
    w_qkv_r = jnp.concatenate([w[:, :three] for w in attn_r], axis=1)
    w_out_r = jnp.concatenate([w[:, three:] for w in attn_r], axis=1)
    qkv = (dot_nn(x_full, w_qkv_r) + v1["qkv"]).astype(BF)
    qkv = advance(qkv, one_m)
    qkv, *two.state = tie(qkv, *two.state)
    qkv = launch(qkv, two)
    attended = attn_fwd(seg_counts, qkv)
    while one_m.left() > 1:
        attended = advance(attended, one_m)
    attended = advance(attended, two)
    partial_attn = dot_nt(attended, w_out_r).astype(BF)
    first_sum = (
        partial_attn[:half].astype(F32)
        + swap_half(partial_attn[half:]).astype(F32)
        + v1["attn"]
        + x_own.astype(F32)
    )
    unit_one, inv_one = norm_stats(first_sum)
    first = unit_one * v1["gain_one"] + v1["shift_one"]
    first_low = first.astype(BF)
    first_full = jnp.concatenate([first_low, swap_half(first_low)], axis=0)
    first_full = settle(first_full, one_m)
    w_up_r, w_down_r, two_attn_r = one_m.results()
    act, slope = up_gelu(first_full, w_up_r, v1["hidden"])
    while two.left() > 3:
        act = advance(act, two)
    act = advance(act, two)
    partial_mlp = dot_nt(act, w_down_r).astype(BF)
    second_sum = (
        partial_mlp[:half].astype(F32) + swap_half(partial_mlp[half:]).astype(F32) + v1["mlp"] + first
    )
    while two.left() > 1:
        second_sum = advance(second_sum, two)
    unit_two, inv_two = norm_stats(second_sum)
    first_out = unit_two * v1["gain_two"] + v1["shift_two"]

    row_in = lax.broadcasted_iota(jnp.int32, (half, 1), 0)
    valid = part * half + row_in < length
    is_cls = lax.broadcasted_iota(jnp.int32, (1, SEG, 1), 1) == 0

    def with_cls(rows, cls):
        return jnp.where(is_cls, cls[:, None, :], rows.reshape(seg_half, SEG, dim)).reshape(half, dim)

    cot = jnp.where(valid, cotangent[0], jnp.zeros_like(cotangent[0]))
    grad_y_low = dot_nn(cot, perm).astype(BF)
    grad_out = with_cls(grad_y_low.astype(F32), jnp.zeros((seg_half, dim), F32))
    g_second = norm_bwd(grad_out, unit_two, inv_two, v1["gain_two"])
    g_second_low = g_second.astype(BF)
    g_mlp = jnp.concatenate([g_second_low, swap_half(g_second_low)], axis=0)
    gpre = (dot_nn(g_mlp, w_down_r) * slope.astype(F32)).astype(BF)
    part_h = dot_nt(gpre, w_up_r).astype(BF)
    gw_up = dot_tn(first_full, gpre).astype(BF)
    gw_down = dot_tn(g_mlp, act).astype(BF)
    g_first = part_h[:half].astype(F32) + swap_half(part_h[half:]).astype(F32) + g_second
    g_first_sum = norm_bwd(g_first, unit_one, inv_one, v1["gain_one"])
    g_first_low = g_first_sum.astype(BF)
    g_attn = jnp.concatenate([g_first_low, swap_half(g_first_low)], axis=0)
    g_attended = dot_nn(g_attn, w_out_r).astype(BF)
    gw_out = dot_tn(g_attn, attended).astype(BF)
    early = Scatter([[gw_up], [gw_down]], orders[1:], bits, count)
    g_attended = launch(g_attended, early)

    sums_own = jnp.concatenate([firsts(second_sum), firsts(first_sum)], axis=0)
    sums_other = swap_half(sums_own)
    second_sum_1 = padded(turned(jnp.concatenate([sums_own[:seg_half], sums_other[:seg_half]], axis=0)))
    first_sum_1 = padded(turned(jnp.concatenate([sums_own[seg_half:], sums_other[seg_half:]], axis=0)))
    unit_two_1, inv_two_1 = norm_stats(second_sum_1)
    unit_one_1, inv_one_1 = norm_stats(first_sum_1)
    first_low_1 = (unit_one_1 * v1["gain_one"] + v1["shift_one"]).astype(BF)
    act_1, slope_1, att_1 = (turned(firsts(v)) for v in (act, slope, attended))
    cls_rel = unit_two_1 * v1["gain_two"] + v1["shift_two"]
    cls_in = padded(cls_rel[:segments] + seg_rows)
    g_c = padded(both_halves(firsts(grad_y_low))).astype(F32)

    cls_in, g_attended, gw_out = tie(cls_in, g_attended, gw_out)
    cls_in = settle(cls_in, two)
    attn_w = [(two_attn_r, p) for p in span]
    up_w, down_w = ([(w, p) for p in span] for w in two.results())
    cls_low = cls_in.astype(BF)
    rows_c = cls_in.shape[0]
    qkv_c, att_c, part_c = cls_call(
        cls_attn_kernel, "cls_attn", cls_count, cls_low, attn_w, tile, v2["qkv"],
        [((rows_c, 3 * width), BF), ((segments, width), BF), ((rows_c, dim), F32)],
    )
    sum_c1 = part_c + swap_half(part_c) + v2["attn"] + cls_in
    unit_c1, inv_c1 = norm_stats(sum_c1)
    first_c = unit_c1 * v2["gain_one"] + v2["shift_one"]
    first_c_low = first_c.astype(BF)
    act_c, slope_c, part_c2 = cls_call(
        cls_up_kernel, "cls_up", None, first_c_low, up_w + down_w, tile, v2["hidden"],
        [((segments, hidden), BF), ((rows_c, hidden), F32), ((rows_c, dim), F32)],
    )
    sum_c2 = part_c2 + swap_half(part_c2) + v2["mlp"] + first_c
    unit_c2, inv_c2 = norm_stats(sum_c2)
    cls_out = unit_c2 * v2["gain_two"] + v2["shift_two"]
    combined = jnp.where(valid, with_cls(first_out, own_half(cls_out)), 0.0).astype(BF)
    output = dot_nn(combined, perm).astype(BF)[None]

    g_second_c = norm_bwd(g_c, unit_c2, inv_c2, v2["gain_two"])
    g_mlp_c = g_second_c.astype(BF)
    back_outs = [((segments, hidden), BF), ((rows_c, dim), F32)]
    gpre_c, part_g1 = cls_call(
        cls_up_back_kernel, "cls_up_back", None, g_mlp_c, up_w + down_w, tile, slope_c, back_outs
    )
    g_first_c = part_g1 + swap_half(part_g1) + g_second_c
    g_sum_c = norm_bwd(g_first_c, unit_c1, inv_c1, v2["gain_one"])
    g_attn_c = g_sum_c.astype(BF)
    gqkv_c, part_g2 = cls_call(
        cls_attn_back_kernel, "cls_attn_back", cls_count, g_attn_c, attn_w, tile, qkv_c,
        [((segments, 3 * width), BF), ((rows_c, dim), F32)],
    )
    g_cls_in = part_g2 + swap_half(part_g2) + g_sum_c
    near_two = tuple(f[:segments] for f in (cls_low, first_c_low, g_attn_c, g_mlp_c))
    far_two = (act_c, gpre_c, att_c, gqkv_c) + near_two
    wide_two = Gather([jnp.concatenate(far_two, axis=1)], orders[:1], bits, count)
    while early.left() > 3:
        g_cls_in = advance(g_cls_in, early)
    g_cls_in = launch(g_cls_in, wide_two)

    g_second_1 = norm_bwd(g_cls_in, unit_two_1, inv_two_1, v1["gain_two"])
    g_mlp_1 = g_second_1.astype(BF)
    gpre_1, part_1 = cls_call(
        cls_up_back_kernel, "cls_up_back", None, g_mlp_1, [(w, p) for w in (w_up_r, w_down_r) for p in span], tile,
        padded(slope_1.astype(F32)), back_outs
    )
    part_1 = advance(part_1, wide_two)
    g_first_1 = part_1 + swap_half(part_1) + g_second_1
    g_sum_1 = norm_bwd(g_first_1, unit_one_1, inv_one_1, v1["gain_one"])
    g_attn_1 = g_sum_1.astype(BF)
    g_att_1 = turned(dot_nn(g_attn_1, w_out_r).astype(BF)[:segments])

    near_one = tuple(f[:segments] for f in (first_low_1, g_mlp_1, g_attn_1))
    far_one = (act_1, gpre_1, att_1) + near_one
    wide_one = Gather([jnp.concatenate(far_one, axis=1)], orders[1:2], bits, count)
    g_att_1 = advance(g_att_1, early, wide_two)
    g_att_1 = launch(g_att_1, wide_one)

    scale_one = 1.0 / math.sqrt(seqs_here * count * full_len)
    scale_two = 1.0 / math.sqrt(seqs_here * count * segments)

    def spread(values, total):
        zero = jnp.zeros((total - values.shape[0],), F32)
        return jnp.where(part == 0, jnp.concatenate([values, zero]), jnp.concatenate([zero, values]))

    def both_sums(rows, cls):
        return (column_sum(rows) + column_sum(own_half(cls))) * scale_one

    def cls_sums(cls):
        return column_sum(own_half(cls)) * scale_two

    sums_c = column_sum(gqkv_c.astype(F32)).reshape(PIECES, 3, PAIR) * scale_two
    rel_rows = jnp.stack(
        [
            both_sums(g_first_sum, g_sum_1),
            both_sums(g_second, g_second_1),
            both_sums(g_first, g_first_1),
            both_sums(grad_out, g_cls_in),
            cls_sums(g_sum_c),
            cls_sums(g_second_c),
            cls_sums(g_first_c),
            cls_sums(g_c),
            both_sums(g_first * unit_one, g_first_1 * unit_one_1),
            both_sums(grad_out * unit_two, g_cls_in * unit_two_1),
            cls_sums(g_first_c * unit_c1),
            cls_sums(g_c * unit_c2),
        ]
    )
    zeros_half = jnp.zeros((seg_half, dim), F32)
    cls_part = own_half(g_cls_in) * scale_two
    seg_grad = jnp.where(
        part == 0,
        jnp.concatenate([cls_part, zeros_half], axis=0),
        jnp.concatenate([zeros_half, cls_part], axis=0),
    )
    up_rows = jnp.stack(
        [
            spread((dot_nn(jnp.ones((16, 2 * half), BF), gpre)[0] + column_sum(gpre_1.astype(F32))) * scale_one, hidden_all),
            spread(column_sum(gpre_c.astype(F32)) * scale_two, hidden_all),
        ]
    )
    per_row = 2 * hidden_all // dim
    by_owner = up_rows.reshape(2, count, -1).transpose(1, 0, 2).reshape(dim, per_row)
    plain_rows = jnp.stack([spread(sums_c[:, k].reshape(-1), dim) for k in (0, 2)])
    canon = dot_exact(jnp.concatenate([plain_rows, by_owner.T], axis=0), perm_f)
    small_rows = jnp.concatenate([rel_rows, seg_grad, canon], axis=0)
    small_rows = small_rows + swap_tensor(small_rows)
    filler = jnp.zeros((PAIR - small_rows.shape[0] - 2, dim), F32)
    small_cols = jnp.concatenate([small_rows, filler], axis=0).T.astype(BF)
    g_att_1, small_cols, output = tie(g_att_1, small_cols, output)

    gqkv, gqkv_sums = attn_bwd(seg_counts, qkv, g_attended, g_att_1)
    gw_qkv = dot_tn(x_full, gqkv).astype(BF)
    sums_o = gqkv_sums.reshape(PIECES, 3, PAIR) * scale_one
    bias_own = jnp.stack([spread(sums_o[:, k].reshape(-1), dim) for k in (0, 2)])
    bias_cols = dot_exact(bias_own + swap_tensor(bias_own), perm_f).T.astype(BF)
    small_cols = jnp.concatenate([small_cols, bias_cols], axis=1)
    late = Scatter(
        [[cut(gw_qkv, three, p), cut(gw_out, PAIR, p)] + [small_cols] * (p == 0) for p in span], orders, bits, count
    )
    gqkv = launch(gqkv, late)
    wides = (wide_two, wide_one)
    gqkv = advance(gqkv, early, wide_one)
    part_x = dot_nt(gqkv, w_qkv_r).astype(BF)

    part_x = advance(part_x, late, wide_two)
    part_x = advance(part_x, wide_one)
    g_first_all = with_cls(g_first_sum, own_half(g_sum_1))
    g_in = part_x[:half].astype(F32) + swap_half(part_x[half:]).astype(F32) + g_first_all
    g_in_high = lax.reduce_precision(g_in, 8, 7)
    grad_input = (dot_nn(g_in_high.astype(BF), perm) + dot_nn((g_in - g_in_high).astype(BF), perm))[None]
    anchor = jnp.zeros((), F32)
    movers = (late, early, *wides)
    while any(m.left() > 1 for m in movers):
        for m in movers:
            if m.left() > 1:
                anchor = advance(anchor, m)
    anchor = settle(anchor, late, early, *wides)

    shape = (width, hidden, dim, chunk, segments, scale_one, scale_two)
    grad_three, grad_last, grad_w_up, grad_down, small_own = owner_sums(
        shape, wide_two.results()[0], wide_one.results()[0], early.pairs() + late.pairs()
    )
    grad_w_qkv = grad_three.reshape(2, chunk, 3, width)
    grad_w_out = grad_last.transpose(0, 2, 1)
    grad_w_down = grad_down.transpose(0, 2, 1)

    mine = small_own.T
    rows_own = jnp.where(part == 0, mine[:, :piece], mine[:, piece:])
    vecs = rows_own[:12]
    grad_vec = jnp.concatenate([rows_own[PAIR - 2 :], vecs[:4], rows_own[20:22], vecs[4:8]], axis=0).reshape(2, 6, piece)
    grad_gain = vecs[8:].reshape(2, 2, piece)
    grad_seg = rows_own[12:20]
    up_own = mine[22 : 22 + per_row].T.reshape(2, 2, piece_up)
    grad_up_vec = jnp.where(part == 0, up_own[:, 0], up_own[:, 1])
    return (
        output,
        grad_input,
        grad_w_qkv,
        grad_w_out,
        grad_w_up,
        grad_w_down,
        grad_vec,
        grad_gain,
        grad_up_vec,
        grad_seg,
    )


def solution(mesh):
    return jax.shard_map(
        local,
        mesh=mesh,
        in_specs=(
            P("dp", "tensor", None),
            P("dp", "tensor", None),
            P("dp"),
            P(None, "dp", None, "tensor"),
            P(None, "tensor", "dp"),
            P(None, "dp", "tensor"),
            P(None, "tensor", "dp"),
            P(None, None, ("dp", "tensor")),
            P(None, None, ("dp", "tensor")),
            P(None, ("dp", "tensor")),
            P(None, ("dp", "tensor")),
        ),
        out_specs=(
            P("dp", "tensor", None),
            P("dp", "tensor", None),
            P(None, "dp", None, "tensor"),
            P(None, "tensor", "dp"),
            P(None, "dp", "tensor"),
            P(None, "tensor", "dp"),
            P(None, None, ("dp", "tensor")),
            P(None, None, ("dp", "tensor")),
            P(None, ("dp", "tensor")),
            P(None, ("dp", "tensor")),
        ),
        check_vma=False,
    )
```
